32 devices in a mesh: grp: 2 (over x), tile: 8 (over z, y), wave: 2 (over core).
Axes of the slice: x: 2, y: 2, z: 4, core: 2. Of those that a mesh axis runs over, the one named last changes fastest.
Arguments:
- residual: float32 [16, 8, 2, 8, 128], P(('grp', 'tile'), 'wave'), parts along dimension 0, may hold values from -210 to 210
- kernel: bfloat16 [16, 8, 9, 2, 128, 128], P(('grp', 'tile'), 'wave'), parts along dimension 0, may hold values from -0.125 to 0.125
- offsets: float32 [16, 8, 2, 128], P(('grp', 'tile'), 'wave'), parts along dimension 0, may hold values from 0 to 1
- neighbor: int32 [16, 8, 9], P(('grp', 'tile'), 'wave'), parts along dimension 0, may hold values from 0 to 8, each once within a row
- frequency: int32 [16], P('grp'), parts along dimension 0, may hold values from 0 to 7, each once
- lattice_x: int32 [128], replicated, may hold values from 0 to 127, each once
- lattice_y: int32 [128], replicated, may hold values from 0 to 127, each once
- spectral_weight: float32 [8, 128, 128], replicated, may hold values from 0.1 to 3
Outputs:
- image_two: float32 [16, 8, 2, 8, 128], P(('grp', 'tile'), 'wave'), parts along dimension 0
- arnoldi: float32 [8, 8], P('grp'), parts along dimension 0
The draws below stay inside these ranges and needn't reach their ends.
There are 2 independent parts, one for each index of `grp`. The reference program is written for one: setup_inputs(seed, part) draws one part's arguments, and reference() takes and returns one part's arrays. A program takes and returns all parts, laid end to end along the dimension named above; an argument that names none is the same for every part. Nothing has to cross between parts.
Inputs may be any that keep to these rules, and one draw needn't show every extreme that they name: `neighbor`: each row names each of the nine neighbour slots once. `frequency`: each index appears once. `lattice_x`: each index appears once. `lattice_y`: each index appears once.
All inputs are finite; a program needn't handle non-finite values.
Results may differ from the reference program's by a relative error of at most 0.013.
Values may be sent and summed in bfloat16 or wider, within the bound.
A program may use at most 64 MiB of HBM per device.

```python
import math
import jax
import jax.numpy as jnp
from jax import lax

PANELS_T = 128
VECTORS = 8
MODES_X = 128
MODES_Y = 128
FREQUENCIES = 8
GRID_X = 8
GRID_Y = 8
PANELS = 8192


def draw_residual(key, part):
    key_a, key_b = jax.random.split(key, 2)
    full_shape = (GRID_X, GRID_Y, 2, VECTORS, PANELS_T)
    column = jnp.arange(GRID_X, dtype=jnp.float32)[:, None, None, None, None] / max(GRID_X - 1, 1)
    spread = 10.0 ** jax.random.uniform(key_b, (GRID_X, GRID_Y, 1, 1, PANELS_T), dtype=jnp.float32)
    rising = 3.0 ** column
    values = jnp.clip(jax.random.normal(key_a, full_shape, dtype=jnp.float32), -4.0, 4.0)
    return values * rising * spread


def level_of(key, shape, cuts, least, top_value):
    gain = 1.0
    for dim, parts in cuts:
        heights = jax.random.uniform(jax.random.fold_in(jax.random.fold_in(key, 6), dim), (parts,), jnp.float32, least / len(cuts), top_value / len(cuts))
        gain = gain * jnp.repeat(jnp.exp(heights), shape[dim] // parts).reshape((-1,) + (1,) * (len(shape) - 1 - dim))
    return gain


def gaussian(own_key, shape, scale, most, cuts=(), kind=jnp.bfloat16):
    gain = level_of(own_key, shape, cuts, -0.22, 0.18) if cuts else 1.0
    entries = jax.random.normal(own_key, shape, jnp.float32) * scale * gain
    return jnp.minimum(jnp.maximum(entries, -most), most).astype(kind)


def setup_inputs(seed: int = 0, part: int = 0) -> dict:
    key_list = jax.random.split(jax.random.key(seed), 9)
    part_keys = jax.random.split(jax.random.fold_in(key_list[8], part), 9)
    return {
        "residual": draw_residual(jax.random.fold_in(jax.random.fold_in(key_list[8], part), 71), part),
        "kernel": gaussian(part_keys[1], (GRID_X, GRID_Y, 9, 2, PANELS_T, PANELS_T), (18 * PANELS_T) ** -0.5, 0.125, ((0, 8), (1, 2))),
        "offsets": jnp.clip(1.0 * jax.random.uniform(part_keys[2], (GRID_X, GRID_Y, 2, PANELS_T), jnp.float32) ** level_of(part_keys[2], (GRID_X, GRID_Y, 2, PANELS_T), ((0, 8), (1, 2)), -0.2, 0.2), 0.0, 1.0),
        "neighbor": jax.vmap(lambda own: jax.random.permutation(own, 9))(jax.random.split(part_keys[3], GRID_X * GRID_Y)).reshape((GRID_X, GRID_Y, 9)).astype(jnp.int32),
        "frequency": jax.random.permutation(part_keys[4], FREQUENCIES).astype(jnp.int32),
        "lattice_x": jax.random.permutation(key_list[5], MODES_X).astype(jnp.int32),
        "lattice_y": jax.random.permutation(key_list[6], MODES_Y).astype(jnp.int32),
        "spectral_weight": jnp.clip(jnp.exp(jax.random.uniform(key_list[7], (FREQUENCIES, MODES_X, MODES_Y), jnp.float32, math.log(0.1), math.log(3.0))), 0.1, 3.0),
    }


two_pi = 2.0 * math.pi
eps_norm = 1e-06

def phase_table(position, harmonic):
    phase_angle = two_pi * (position[:, None] * harmonic[None, :])
    return (jnp.cos(phase_angle).astype(jnp.bfloat16), jnp.sin(phase_angle).astype(jnp.bfloat16))

def project_rows(cosine_cols, sine_cols, twisted):
    row_count = cosine_cols.shape[1]
    stacked = jnp.concatenate([cosine_cols, sine_cols], 1)
    gram_matrix = lax.dot_general(stacked, twisted, (((0,), (0,)), ((), ())), preferred_element_type=jnp.float32)
    gram_matrix = gram_matrix.reshape(2, row_count, 2, -1)
    coef_real = gram_matrix[0, :, 0] + gram_matrix[1, :, 1]
    coef_imag = gram_matrix[0, :, 1] - gram_matrix[1, :, 0]
    return jnp.stack([coef_real, coef_imag], 1)

def expand_rows(cosine_cols, sine_cols, scaled):
    row_count = scaled.shape[0]
    upper_rows = scaled.reshape(row_count, -1)
    lower_rows = jnp.stack([-scaled[:, 1], scaled[:, 0]], 1).reshape(row_count, -1)
    matrix = jnp.concatenate([upper_rows, lower_rows], 0)
    stacked = jnp.concatenate([cosine_cols, sine_cols], 1)
    return jnp.dot(stacked, matrix, preferred_element_type=jnp.float32)

def twist_density(panel_density, cosine_y, sine_y):
    density_real = panel_density[:, 0, :, None].astype(jnp.float32)
    density_imag = panel_density[:, 1, :, None].astype(jnp.float32)
    wave_cos = cosine_y.astype(jnp.float32)[:, None, :]
    wave_sin = sine_y.astype(jnp.float32)[:, None, :]
    part_real = wave_cos * density_real + wave_sin * density_imag
    part_imag = wave_cos * density_imag - wave_sin * density_real
    return jnp.stack([part_real, part_imag], 1).reshape(panel_density.shape[0], -1).astype(jnp.bfloat16)

def finish(summed, cosine_y, sine_y, vectors):
    shaped = summed.reshape(summed.shape[0], 2, vectors, -1)
    wave_cos = cosine_y.astype(jnp.float32)[:, None, :]
    wave_sin = sine_y.astype(jnp.float32)[:, None, :]
    far_real = lax.optimization_barrier(jnp.sum(shaped[:, 0] * wave_cos - shaped[:, 1] * wave_sin, -1))
    far_imag = lax.optimization_barrier(jnp.sum(shaped[:, 0] * wave_sin + shaped[:, 1] * wave_cos, -1))
    return jnp.stack([far_real, far_imag], 1)

def combine_near(product, vectors):
    first_half = product[:, 0]
    second = product[:, 1]
    near_real = first_half[:, :vectors] - second[:, vectors:]
    near_imag = second[:, :vectors] + first_half[:, vectors:]
    return jnp.stack([near_real, near_imag], 1)

def panel_sum(values):
    return lax.optimization_barrier(jnp.sum(values, axis=(0, 1, 3)))

def reference(residual, kernel, offsets, neighbor, frequency, lattice_x, lattice_y, spectral_weight):
    column = jnp.arange(GRID_X, dtype=jnp.float32)
    row_index = jnp.arange(GRID_Y, dtype=jnp.float32)
    position_x = ((column[:, None, None] + offsets[:, :, 0, :]) / GRID_X).reshape(-1)
    position_y = ((row_index[None, :, None] + offsets[:, :, 1, :]) / GRID_Y).reshape(-1)
    harmonic_x = (lattice_x - MODES_X // 2).astype(jnp.float32)
    harmonic_y = (lattice_y - MODES_Y // 2).astype(jnp.float32)
    cosine_x, sine_x = phase_table(position_x, harmonic_x)
    cosine_y, sine_y = phase_table(position_y, harmonic_y)
    weight_rows = jnp.take(spectral_weight, frequency[:VECTORS].astype(jnp.int32), axis=0)
    factor = weight_rows * (1.0 / math.sqrt(MODES_X * MODES_Y * PANELS))
    factor_wide = jnp.transpose(factor, (1, 0, 2)).reshape(MODES_X, VECTORS * MODES_Y)[:, None, :]

    def near_field(density):
        candidates = []
        for slot_index in range(9):
            shift_x = slot_index // 3 - 1
            shift_y = slot_index % 3 - 1
            candidates.append(jnp.roll(density, (-shift_x, -shift_y), axis=(0, 1)))
        stacked = jnp.stack(candidates, 2).reshape(GRID_X * GRID_Y, 9, -1)
        picked = jnp.take_along_axis(stacked, neighbor.reshape(GRID_X * GRID_Y, 9, 1), axis=1)
        picked = picked.reshape(GRID_X * GRID_Y, 9, 2 * VECTORS, PANELS_T)
        blocks = kernel.reshape(GRID_X * GRID_Y, 9, 2, PANELS_T, PANELS_T)
        product = jnp.einsum('tjmp,tjcpq->tcmq', picked.astype(jnp.float32), blocks.astype(jnp.float32))
        return combine_near(product, VECTORS).reshape(GRID_X, GRID_Y, 2, VECTORS, PANELS_T)

    def far_field(density):
        panel_density = jnp.transpose(density, (0, 1, 4, 2, 3)).reshape(PANELS, 2, VECTORS)
        twisted = twist_density(panel_density, cosine_y, sine_y)
        coeffs = project_rows(cosine_x, sine_x, twisted)
        scaled = (coeffs * factor_wide).astype(jnp.bfloat16)
        summed = expand_rows(cosine_x, sine_x, scaled)
        far_panel = finish(summed, cosine_y, sine_y, VECTORS)
        return far_panel.reshape(GRID_X, GRID_Y, PANELS_T, 2, VECTORS).transpose(0, 1, 3, 4, 2)

    def apply_operator(density):
        return 0.5 * density.astype(jnp.float32) + near_field(density) + far_field(density)
    squares = panel_sum(residual[:, :, 0] * residual[:, :, 0] + residual[:, :, 1] * residual[:, :, 1])
    basis_scale = jnp.sqrt(squares / PANELS + eps_norm)
    basis_one = (residual / basis_scale[None, None, None, :, None]).astype(jnp.bfloat16)
    image_one = apply_operator(basis_one)
    basis_real = basis_one[:, :, 0].astype(jnp.float32)
    basis_imag = basis_one[:, :, 1].astype(jnp.float32)
    image_real = image_one[:, :, 0]
    image_imag = image_one[:, :, 1]
    coef_real = panel_sum(basis_real * image_real + basis_imag * image_imag) / PANELS
    coef_imag = panel_sum(basis_real * image_imag - basis_imag * image_real) / PANELS
    wide_real = coef_real[None, None, :, None]
    wide_imag = coef_imag[None, None, :, None]
    update_real = image_real - (wide_real * basis_real - wide_imag * basis_imag)
    update_imag = image_imag - (wide_real * basis_imag + wide_imag * basis_real)
    update_sq = panel_sum(update_real * update_real + update_imag * update_imag)
    update_scale = jnp.sqrt(update_sq / PANELS + eps_norm)
    next_basis = (jnp.stack([update_real, update_imag], 2) / update_scale[None, None, None, :, None]).astype(jnp.bfloat16)
    image_two = apply_operator(next_basis)
    arnoldi = jnp.stack([basis_scale, coef_real, coef_imag, update_scale])
    return (image_two, arnoldi)
```

```python
import functools
import math

import jax
import jax.numpy as jnp
from jax import lax
from jax.experimental import pallas as pl
from jax.experimental.pallas import tpu as pltpu
from jax.sharding import PartitionSpec as P

eps_norm = 1e-06
f32 = jnp.float32
bf16 = jnp.bfloat16
MESH = pl.DeviceIdType.MESH
phase_a, phase_n, phase_z, phase_f = range(4)

cos_poly = (
    0.9999999890754361,
    -19.739204500992756,
    64.93911749755512,
    -85.45013994334624,
    60.167632824407875,
    -25.967602439336652,
    6.528658637171564,
)
sin_poly = (
    6.283185302518495,
    -41.3417004059728,
    81.60513140266713,
    -76.70301552901445,
    42.02592777896992,
    -14.89984800704947,
    3.2381376825656845,
)


def horner(coefs, z):
    total = coefs[-1] * z + coefs[-2]
    for c in coefs[-3::-1]:
        total = total * z + c
    return total


def cos_sin(turns):
    r = turns - jnp.round(turns)
    z = r * r
    return horner(cos_poly, z), r * horner(sin_poly, z)


def rows_dot(a, b, precision=None):
    return lax.dot_general(
        a, b, (((1,), (1,)), ((), ())), precision=precision, preferred_element_type=f32
    )


def body(
    size_t,
    size_w,
    tiles,
    vectors,
    modes_x,
    modes_y,
    residual,
    blocks,
    offsets,
    neighbor,
    frequency,
    lattice_x,
    lattice_y,
    weight,
    image_out,
    arnoldi_out,
    send_a,
    recv_a,
    send_n,
    recv_n,
    send_z,
    recv_z,
    send_f,
    recv_f,
    send_g1,
    recv_g1,
    send_g2,
    recv_g2,
    halo_1,
    halo_2,
    table_x,
    table_y,
    wide_y,
    phi,
    dense,
    zeta,
    far,
    fact,
    kernel_vmem,
    weight_vmem,
    load_sem,
    col_send,
    col_recv,
    mate_send,
    mate_recv,
    halo_send,
    halo_recv,
):
    devices = size_t * size_w
    sub = size_t // vectors
    members = size_w * sub
    rows = 2 * tiles
    half_x = modes_x // 2
    half_y = modes_y // 2
    lanes = 128
    panels = devices * tiles * lanes
    count_x = size_t
    count_y = size_w * tiles
    t = lax.axis_index("tile")
    w = lax.axis_index("wave")
    me = t * size_w + w
    mine = t // sub
    part = lax.rem(t, sub)
    member = part * size_w + w

    barrier = pltpu.get_barrier_semaphore()

    def greet(k, carry):
        other = lax.rem(me + k, devices)
        place = {"tile": other // size_w, "wave": lax.rem(other, size_w)}
        pl.semaphore_signal(barrier, inc=1, device_id=place, device_id_type=MESH)
        return carry

    lax.fori_loop(1, devices, greet, 0)
    load_w = pltpu.make_async_copy(weight, weight_vmem, load_sem.at[0])
    load_w.start()
    load_k = pltpu.make_async_copy(blocks, kernel_vmem, load_sem.at[1])
    load_k.start()

    def turn(k):
        return lax.rem(mine + k, vectors)

    def column_copy(phase, k, source, target):
        other = turn(k)
        return pltpu.make_async_remote_copy(
            src_ref=source.at[other],
            dst_ref=target.at[mine],
            send_sem=col_send.at[phase, k],
            recv_sem=col_recv.at[phase, vectors - k],
            device_id={"tile": other * sub + part, "wave": w},
            device_id_type=MESH,
        )

    def column_wait(phase, k, target):
        slot = target.at[turn(k)]
        pltpu.make_async_copy(slot, slot, col_recv.at[phase, k]).wait()

    def mate_copy(phase, k, source, target):
        other = lax.rem(member + k, members)
        return pltpu.make_async_remote_copy(
            src_ref=source,
            dst_ref=target.at[member],
            send_sem=mate_send.at[phase, k],
            recv_sem=mate_recv.at[phase, members - k],
            device_id={"tile": mine * sub + other // size_w, "wave": lax.rem(other, size_w)},
            device_id_type=MESH,
        )

    def mate_wait(phase, k, target):
        slot = target.at[lax.rem(member + k, members)]
        pltpu.make_async_copy(slot, slot, mate_recv.at[phase, k]).wait()

    up = lax.rem(t + 1, size_t)
    down = lax.rem(t + size_t - 1, size_t)
    other_w = lax.rem(w + 1, size_w)

    def halo_copies(phase, halo):
        copies = []
        targets = ((up, w, 0), (up, other_w, 0), (t, other_w, 1), (down, w, 2), (down, other_w, 2))
        for number, (to_t, to_w, row) in enumerate(targets):
            copies.append(
                pltpu.make_async_remote_copy(
                    src_ref=halo.at[1, pl.ds(w * tiles, tiles)],
                    dst_ref=halo.at[row, pl.ds(w * tiles, tiles)],
                    send_sem=halo_send.at[phase, number],
                    recv_sem=halo_recv.at[phase, number],
                    device_id={"tile": to_t, "wave": to_w},
                    device_id_type=MESH,
                )
            )
        return copies

    started = []

    def start(copy):
        copy.start()
        started.append(copy)

    row_id = lax.broadcasted_iota(jnp.int32, (rows, lanes), 0)
    upper = row_id < tiles
    sign = jnp.where(upper, -1.0, 1.0)

    def times_i(x):
        return pltpu.roll(x, tiles, 0) * sign

    offset_rows = jnp.concatenate([offsets[:, 0, :], offsets[:, 1, :]], 0)
    for h in range(tiles):
        rounded = []
        for c in range(2):
            value = residual[h, c]
            send_a[:, c * tiles + h, :] = value
            rounded.append(value.astype(bf16))
        halo_1[1, w * tiles + h] = jnp.concatenate(rounded, 0)
    for v in range(vectors):
        send_a[v, rows : 2 * rows, :] = offset_rows
    recv_a[mine] = send_a[mine]

    low_x = lax.broadcasted_iota(jnp.int32, (8, lanes), 0).astype(f32) + 0.5
    high_x = lax.broadcasted_iota(jnp.int32, (8, lanes), 0).astype(f32) * 8.0
    count = jnp.where(upper, float(count_x), float(count_y))
    tile_row = (row_id - tiles + w * tiles).astype(f32)

    def harmonics(position):
        cos_l, sin_l = cos_sin(position * low_x)
        cos_h, sin_h = cos_sin(position * high_x)
        cosines, sines = [], []
        for m in range(8):
            c = jnp.broadcast_to(cos_h[m : m + 1], (8, lanes))
            s = jnp.broadcast_to(sin_h[m : m + 1], (8, lanes))
            cosines.append(c * cos_l - s * sin_l)
            sines.append(s * cos_l + c * sin_l)
        return jnp.concatenate(cosines + sines, 0)

    def tables(k):
        u = turn(k)
        off = recv_a[u, rows : 2 * rows, :]
        strip = (u * sub + part).astype(f32)
        pos = (jnp.where(upper, strip, tile_row) + off) / count
        cos_p, sin_p = cos_sin(0.5 * (pos + pltpu.roll(pos, tiles, 0)))
        phi[k, 0] = cos_p
        phi[k, 1] = sin_p
        for h in range(tiles):
            cols = slice(h * lanes, (h + 1) * lanes)
            tx = harmonics(jnp.broadcast_to(pos[h : h + 1], (8, lanes)))
            table_x[k, :, cols] = tx.astype(bf16)
            ty = harmonics(jnp.broadcast_to(pos[tiles + h : tiles + h + 1], (8, lanes)))
            table_y[k, :, cols] = ty.astype(bf16)
            wide_y[k, :, cols] = ty

    def project(k, density):
        rotated = density * phi[k, 0] + times_i(density) * phi[k, 1]
        twisted = []
        for h in range(tiles):
            cols = slice(h * lanes, (h + 1) * lanes)
            ty = table_y[k, :, cols]
            both = []
            for c in range(2):
                row = c * tiles + h
                q = jnp.broadcast_to(rotated[row : row + 1], (16, lanes)).astype(bf16)
                both.append(ty * jnp.concatenate([q] * (modes_y // 16), 0))
            twisted.append(jnp.concatenate(both, 0))
        return rows_dot(jnp.concatenate(twisted, 1), table_x[k])

    def weighted(total):
        x_r, y_r = total[0:half_y], total[half_y:modes_y]
        x_i, y_i = total[modes_y : modes_y + half_y], total[modes_y + half_y :]
        rx_r, ry_r, rx_i, ry_i = [pltpu.roll(x, half_x, 1) for x in (x_r, y_r, x_i, y_i)]
        f_0 = fact[0:half_y, 0:modes_x]
        f_s = fact[0:half_y, modes_x:]
        f_t = fact[half_y:, 0:modes_x]
        f_1 = fact[half_y:, modes_x:]
        return jnp.concatenate(
            [
                f_0 * x_r + f_1 * ry_r - f_s * rx_i + f_t * y_i,
                f_0 * y_r - f_1 * rx_r - f_t * x_i - f_s * ry_i,
                f_0 * x_i + f_1 * ry_i + f_s * rx_r - f_t * y_r,
                f_0 * y_i - f_1 * rx_i + f_t * x_r + f_s * ry_r,
            ],
            0,
        ).astype(bf16)

    def expand(k, matrix):
        for h in range(tiles):
            cols = slice(h * lanes, (h + 1) * lanes)
            summed = jnp.dot(matrix, table_x[k, :, cols], preferred_element_type=f32)
            ty = wide_y[k, :, cols]
            for c in range(2):
                row = c * tiles + h
                far[k, row : row + 1, :] = jnp.sum(
                    summed[c * modes_y : (c + 1) * modes_y] * ty, 0, keepdims=True
                )
        value = far[k]
        return value * phi[k, 0] - times_i(value) * phi[k, 1]

    def near_field(halo):
        result = []
        for h in range(tiles):
            picked = []
            for j in range(9):
                slot = neighbor[0, h, j]
                row = slot // 3
                column = lax.rem(w * tiles + h + lax.rem(slot, 3) - 1 + count_y, count_y)
                picked.append(halo[row, column])
            left = jnp.concatenate(picked, 1)
            right = jnp.concatenate(
                [
                    jnp.concatenate([kernel_vmem[h, j, c] for j in range(9)], 0)
                    for c in range(2)
                ],
                1,
            )
            product = jnp.dot(left, right, preferred_element_type=f32)
            result.append(
                (
                    product[:vectors, :lanes] - product[vectors:, lanes:],
                    product[:vectors, lanes:] + product[vectors:, :lanes],
                )
            )
        return result

    pl.semaphore_wait(barrier, devices - 1)
    copies_1 = halo_copies(0, halo_1)
    for k in range(1, vectors):
        start(column_copy(phase_a, k, send_a, recv_a))
    for copy in copies_1:
        start(copy)

    tables(0)

    load_w.wait()
    my_weight = weight_vmem[frequency[mine]] * (1.0 / math.sqrt(modes_x * modes_y * panels))
    diagonal = jnp.sum(jnp.sum(my_weight, 0, keepdims=True), 1, keepdims=True)
    exact = lax.Precision.HIGHEST

    def pick(lattice, half):
        index = lax.broadcasted_iota(jnp.int32, (half, 2 * half), 0)
        given = jnp.broadcast_to(lattice[...], index.shape)
        plus = jnp.where(given == index + half, 1.0, 0.0)
        minus = jnp.where(given == half - 1 - index, 1.0, 0.0)
        return plus + minus, plus - minus

    even_y, odd_y = pick(lattice_y, half_y)
    even_x, odd_x = pick(lattice_x, half_x)
    by_y = rows_dot(jnp.concatenate([even_y, odd_y], 0), my_weight, exact)
    pick_x = jnp.concatenate([even_x, even_x, -odd_x, odd_x], 0)
    fact[...] = rows_dot(by_y, pick_x, exact)

    def send_tiles(pairs, slab):
        for h in range(tiles):
            for c in range(2):
                slab[:, c * tiles + h, :] = pairs[h][c]

    load_k.wait()
    for copy in copies_1:
        copy.wait_recv()
    send_tiles(near_field(halo_1), send_n)
    recv_n[mine] = send_n[mine]
    for k in range(1, vectors):
        start(column_copy(phase_n, k, send_n, recv_n))

    total = None
    for k in range(vectors):
        if k:
            column_wait(phase_a, k, recv_a)
            tables(k)
        dense[k] = recv_a[turn(k), 0:rows, :].astype(bf16).astype(f32)
        term = project(k, dense[k])
        total = term if total is None else total + term

    def gather_sum(phase, source, target):
        if members == 2:
            return source[...] + target[lax.rem(member + 1, members)]
        target[member] = source[...]
        return jnp.sum(target[...], 0)

    send_g1[...] = total
    for k in range(1, members):
        start(mate_copy(0, k, send_g1, recv_g1))
    for k in range(1, members):
        mate_wait(0, k, recv_g1)
    matrix = weighted(gather_sum(0, send_g1, recv_g1))

    for k in range(1, vectors):
        column_wait(phase_n, k, recv_n)

    total = None
    zero = jnp.zeros((rows, lanes), f32)
    sums = [zero] * 5
    for k in range(vectors):
        u = turn(k)
        given = recv_a[u, 0:rows, :]
        base = dense[k]
        value = expand(k, matrix) + recv_n[u] - diagonal * base
        zeta[k] = value
        turned = times_i(value)
        terms = (given * given, base * base, base * value, -base * turned, value * value)
        sums = [x + y for x, y in zip(sums, terms)]
        if k:
            send_z[u] = value
            start(column_copy(phase_z, k, send_z, recv_z))
        else:
            recv_z[mine] = value
        term = project(k, value)
        total = term if total is None else total + term

    send_g2[0 : 2 * modes_y] = total
    line = jnp.zeros((rows, lanes), f32)
    for number, x in enumerate(sums):
        whole = jnp.sum(jnp.sum(x, 0, keepdims=True), 1, keepdims=True)
        line = jnp.where(row_id == number, whole, line)
    send_g2[2 * modes_y :] = line
    for k in range(1, members):
        start(mate_copy(1, k, send_g2, recv_g2))

    for k in range(1, vectors):
        column_wait(phase_z, k, recv_z)
    for h in range(tiles):
        halo_2[1, w * tiles + h] = jnp.concatenate(
            [recv_z[:, c * tiles + h, :].astype(bf16) for c in range(2)], 0
        )
    copies_2 = halo_copies(1, halo_2)
    for copy in copies_2:
        start(copy)

    for k in range(1, members):
        mate_wait(1, k, recv_g2)
    total = gather_sum(1, send_g2, recv_g2)
    matrix = weighted(total[0 : 2 * modes_y])
    line = total[2 * modes_y :]
    squares, base_sq, inner_r, inner_i, value_sq = [line[i : i + 1] for i in range(5)]
    shift = 0.5 + diagonal
    variance = squares / panels + eps_norm
    scale = jnp.sqrt(variance)
    over = 1.0 / (panels * variance)
    rest_r = (shift * base_sq + inner_r) * over
    coef_i = inner_i * over
    coef_r = rest_r
    move_r = coef_r - shift
    update_sq = (
        value_sq
        - 2.0 * (move_r * inner_r + coef_i * inner_i)
        + (move_r * move_r + coef_i * coef_i) * base_sq
    )
    update_scale = jnp.sqrt(jnp.maximum(update_sq, 0.0) * over + eps_norm)
    inverse = 1.0 / (scale * update_scale)
    result = jnp.zeros((rows, lanes), f32)
    for number, x in enumerate((scale, coef_r, coef_i, update_scale, inverse)):
        result = jnp.where(row_id == number, x, result)

    for k in range(vectors):
        u = turn(k)
        value = zeta[k]
        image = value + shift * dense[k]
        out = expand(k, matrix) + 0.5 * value - move_r * image - coef_i * times_i(image)
        send_f[u, 0:rows, :] = out * inverse
        send_f[u, rows : 2 * rows, :] = result
        if k:
            start(column_copy(phase_f, k, send_f, recv_f))
        else:
            recv_f[mine] = send_f[mine]

    for copy in copies_2:
        copy.wait_recv()
    near = near_field(halo_2)
    for k in range(1, vectors):
        column_wait(phase_f, k, recv_f)
    scaling = recv_f[:, rows + 4, :]
    for h in range(tiles):
        for c in range(2):
            image_out[h, c] = recv_f[:, c * tiles + h, :] + near[h][c] * scaling
    row = lax.broadcasted_iota(jnp.int32, (vectors, lanes), 0)
    lane = lax.broadcasted_iota(jnp.int32, (vectors, lanes), 1)
    for number in range(4):
        value = recv_f[:, rows + number, :]
        line = jnp.sum(jnp.where(row == lane, value, 0.0), 0, keepdims=True)
        arnoldi_out[number : number + 1, :] = line[:, :vectors]

    for copy in started:
        copy.wait_send()


def hand_over(image, arnoldi, image_out, arnoldi_out):
    image_out[...] = image[...]
    arnoldi_out[...] = arnoldi[...]


def per_device(
    size_t,
    size_w,
    residual,
    kernel,
    offsets,
    neighbor,
    frequency,
    lattice_x,
    lattice_y,
    spectral_weight,
):
    strips, tiles, _, vectors, lanes = residual.shape
    modes_x, modes_y = spectral_weight.shape[1:]
    assert strips == 1 and lanes == 128 and size_w == 2 and size_t > 2
    assert size_t % vectors == 0 and tiles == 4 and vectors == 8
    assert modes_x == 128 and modes_y == 128
    members = size_w * (size_t // vectors)
    rows = 2 * tiles
    vmem = pl.BlockSpec(memory_space=pltpu.VMEM)
    smem = pl.BlockSpec(memory_space=pltpu.SMEM)
    anywhere = pl.BlockSpec(memory_space=pl.ANY)
    halo = pltpu.VMEM((3, size_w * tiles, 2 * vectors, lanes), bf16)
    wide = pltpu.VMEM((vectors, 2 * rows, lanes), f32)
    slim = pltpu.VMEM((vectors, rows, lanes), f32)
    image, arnoldi = pl.pallas_call(
        functools.partial(body, size_t, size_w, tiles, vectors, modes_x, modes_y),
        out_shape=(
            jax.ShapeDtypeStruct((tiles, 2, vectors, lanes), f32),
            jax.ShapeDtypeStruct((4, vectors), f32),
        ),
        in_specs=[vmem, anywhere, vmem, smem, smem, vmem, vmem, anywhere],
        out_specs=(vmem, vmem),
        scratch_shapes=[
            wide,
            wide,
            slim,
            slim,
            slim,
            slim,
            wide,
            wide,
            pltpu.VMEM((2 * modes_y, modes_x), f32),
            pltpu.VMEM((members, 2 * modes_y, modes_x), f32),
            pltpu.VMEM((2 * modes_y + rows, modes_x), f32),
            pltpu.VMEM((members, 2 * modes_y + rows, modes_x), f32),
            halo,
            halo,
            pltpu.VMEM((vectors, modes_x, tiles * lanes), bf16),
            pltpu.VMEM((vectors, modes_y, tiles * lanes), bf16),
            pltpu.VMEM((vectors, modes_y, tiles * lanes), f32),
            pltpu.VMEM((vectors, 2, rows, lanes), f32),
            slim,
            slim,
            slim,
            pltpu.VMEM((modes_y, 2 * modes_x), f32),
            pltpu.VMEM((tiles, 9, 2, lanes, lanes), bf16),
            pltpu.VMEM(spectral_weight.shape, f32),
            pltpu.SemaphoreType.DMA((2,)),
            pltpu.SemaphoreType.DMA((4, vectors)),
            pltpu.SemaphoreType.DMA((4, vectors)),
            pltpu.SemaphoreType.DMA((2, members)),
            pltpu.SemaphoreType.DMA((2, members)),
            pltpu.SemaphoreType.DMA((2, 5)),
            pltpu.SemaphoreType.DMA((2, 5)),
        ],
        compiler_params=pltpu.CompilerParams(
            collective_id=0, has_side_effects=True, vmem_limit_bytes=56 * 1024 * 1024
        ),
        name="arnoldi_pair",
    )(
        residual[0],
        kernel[0],
        offsets[0],
        neighbor,
        frequency,
        lattice_x[None],
        lattice_y[None],
        spectral_weight,
    )
    image, arnoldi = pl.pallas_call(
        hand_over,
        out_shape=(
            jax.ShapeDtypeStruct(image.shape, f32),
            jax.ShapeDtypeStruct(arnoldi.shape, f32),
        ),
        in_specs=[vmem, vmem],
        out_specs=(vmem, vmem),
        name="hand_over",
    )(image, arnoldi)
    return image[None], arnoldi


def solution(mesh):
    return jax.shard_map(
        functools.partial(per_device, mesh.shape["tile"], mesh.shape["wave"]),
        mesh=mesh,
        in_specs=(
            P(("grp", "tile"), "wave", None, None, None),
            P(("grp", "tile"), "wave", None, None, None, None),
            P(("grp", "tile"), "wave", None, None),
            P(("grp", "tile"), "wave", None),
            P("grp"),
            P(),
            P(),
            P(),
        ),
        out_specs=(P(("grp", "tile"), "wave", None, None, None), P("grp", None)),
        check_vma=False,
    )
```

```python
import functools
import math

import jax
import jax.numpy as jnp
from jax import lax
from jax.experimental import pallas as pl
from jax.experimental.pallas import tpu as pltpu
from jax.sharding import PartitionSpec as P

eps_norm = 1e-06
f32 = jnp.float32
bf16 = jnp.bfloat16
MESH = pl.DeviceIdType.MESH
phase_a, phase_n, phase_z, phase_f, phase_h, phase_o = range(6)

cos_poly = (
    0.9999999890754361,
    -19.739204500992756,
    64.93911749755512,
    -85.45013994334624,
    60.167632824407875,
    -25.967602439336652,
    6.528658637171564,
)
sin_poly = (
    6.283185302518495,
    -41.3417004059728,
    81.60513140266713,
    -76.70301552901445,
    42.02592777896992,
    -14.89984800704947,
    3.2381376825656845,
)


def horner(coefs, z):
    total = coefs[-1] * z + coefs[-2]
    for c in coefs[-3::-1]:
        total = total * z + c
    return total


def cos_sin(turns):
    r = turns - jnp.round(turns)
    z = r * r
    return horner(cos_poly, z), r * horner(sin_poly, z)


def rows_dot(a, b, precision=None):
    return lax.dot_general(
        a, b, (((1,), (1,)), ((), ())), precision=precision, preferred_element_type=f32
    )


def body(
    size_t,
    size_w,
    tiles,
    vectors,
    modes_x,
    modes_y,
    residual_any,
    blocks,
    offsets_any,
    neighbor_any,
    frequency_any,
    lattice_x_any,
    lattice_y_any,
    weight,
    image_out,
    arnoldi_out,
    send_a,
    recv_a,
    send_n,
    recv_n,
    send_z,
    recv_z,
    send_h,
    recv_h,
    send_o,
    recv_o,
    near_h,
    near_o,
    send_f,
    recv_f,
    send_g1,
    recv_g1,
    send_g2,
    recv_g2,
    halo_1,
    halo_2,
    table_x,
    table_y,
    wide_y,
    phi,
    dense,
    zeta,
    far,
    fact,
    residual,
    offsets,
    neighbor,
    frequency,
    lattice_x,
    lattice_y,
    kernel_vmem,
    weight_vmem,
    load_sem,
    col_send,
    col_recv,
    mate_send,
    mate_recv,
    halo_send,
    halo_recv,
):
    devices = size_t * size_w
    sub = size_t // vectors
    members = size_w * sub
    rows = 2 * tiles
    half_x = modes_x // 2
    half_y = modes_y // 2
    lanes = 128
    panels = devices * tiles * lanes
    count_x = size_t
    count_y = size_w * tiles
    t = lax.axis_index("tile")
    w = lax.axis_index("wave")
    me = t * size_w + w
    mine = t // sub
    part = lax.rem(t, sub)
    member = part * size_w + w

    up = lax.rem(t + 1, size_t)
    down = lax.rem(t + size_t - 1, size_t)
    other_w = lax.rem(w + 1, size_w)

    barrier = pltpu.get_barrier_semaphore()

    def greet(to_t, to_w):
        place = {"tile": to_t, "wave": to_w}
        pl.semaphore_signal(barrier, inc=1, device_id=place, device_id_type=MESH)

    if sub == 1:
        greeted = vectors + 2
        greet(up, w)
        greet(down, w)
        for k in range(vectors):
            greet(lax.rem(t + k, size_t), other_w)
    else:
        greeted = devices - 1

        def greet_one(k, carry):
            other = lax.rem(me + k, devices)
            greet(other // size_w, lax.rem(other, size_w))
            return carry

        lax.fori_loop(1, devices, greet_one, 0)

    loads = []
    for number, (source, target) in enumerate(
        (
            (residual_any, residual),
            (offsets_any, offsets),
            (frequency_any, frequency),
            (weight, weight_vmem),
            (lattice_x_any, lattice_x),
            (lattice_y_any, lattice_y),
            (neighbor_any, neighbor),
            (blocks, kernel_vmem),
        )
    ):
        loads.append(pltpu.make_async_copy(source, target, load_sem.at[number]))
        loads[-1].start()

    def turn(k):
        return lax.rem(mine + k, vectors)

    def column_copy(phase, k, source, target, wave=None):
        return pltpu.make_async_remote_copy(
            src_ref=source,
            dst_ref=target.at[mine],
            send_sem=col_send.at[phase, k],
            recv_sem=col_recv.at[phase, (vectors - k) % vectors],
            device_id={"tile": turn(k) * sub + part, "wave": other_w if wave is None else wave},
            device_id_type=MESH,
        )

    def column_wait(phase, k, target):
        slot = target.at[turn(k)]
        pltpu.make_async_copy(slot, slot, col_recv.at[phase, k]).wait()

    def mate_copy(phase, k, source, target):
        other = lax.rem(member + k, members)
        return pltpu.make_async_remote_copy(
            src_ref=source,
            dst_ref=target.at[member],
            send_sem=mate_send.at[phase, k],
            recv_sem=mate_recv.at[phase, members - k],
            device_id={"tile": mine * sub + other // size_w, "wave": lax.rem(other, size_w)},
            device_id_type=MESH,
        )

    def mate_wait(phase, k, target):
        slot = target.at[lax.rem(member + k, members)]
        pltpu.make_async_copy(slot, slot, mate_recv.at[phase, k]).wait()

    def halo_copies(phase, halo):
        copies = []
        targets = ((up, w, 0), (up, other_w, 0), (t, other_w, 1), (down, w, 2), (down, other_w, 2))
        for number, (to_t, to_w, row) in enumerate(targets):
            copies.append(
                pltpu.make_async_remote_copy(
                    src_ref=halo.at[1, pl.ds(w * tiles, tiles)],
                    dst_ref=halo.at[row, pl.ds(w * tiles, tiles)],
                    send_sem=halo_send.at[phase, number],
                    recv_sem=halo_recv.at[phase, number],
                    device_id={"tile": to_t, "wave": to_w},
                    device_id_type=MESH,
                )
            )
        return copies

    started = []

    def start(copy):
        copy.start()
        started.append(copy)

    row_id = lax.broadcasted_iota(jnp.int32, (rows, lanes), 0)
    upper = row_id < tiles
    sign = jnp.where(upper, -1.0, 1.0)

    def times_i(x):
        return pltpu.roll(x, tiles, 0) * sign

    if sub == 1:
        for strip in range(3):
            for h in range(1, tiles - 1):
                halo_2[strip, other_w * tiles + h] = jnp.zeros((2 * vectors, lanes), bf16)
    loads[0].wait()
    loads[1].wait()
    offset_rows = jnp.concatenate([offsets[:, 0, :], offsets[:, 1, :]], 0)
    for h in range(tiles):
        rounded = []
        for c in range(2):
            value = residual[h, c]
            send_a[:, c * tiles + h, :] = value
            rounded.append(value.astype(bf16))
        halo_1[1, w * tiles + h] = jnp.concatenate(rounded, 0)
    for v in range(vectors):
        send_a[v, rows : 2 * rows, :] = offset_rows

    low_x = lax.broadcasted_iota(jnp.int32, (8, lanes), 0).astype(f32) + 0.5
    high_x = lax.broadcasted_iota(jnp.int32, (8, lanes), 0).astype(f32) * 8.0
    count = jnp.where(upper, float(count_x), float(count_y))
    tile_row = (row_id - tiles + other_w * tiles).astype(f32)

    def harmonics(position):
        cos_l, sin_l = cos_sin(position * low_x)
        cos_h, sin_h = cos_sin(position * high_x)
        cosines, sines = [], []
        for m in range(8):
            c = jnp.broadcast_to(cos_h[m : m + 1], (8, lanes))
            s = jnp.broadcast_to(sin_h[m : m + 1], (8, lanes))
            cosines.append(c * cos_l - s * sin_l)
            sines.append(s * cos_l + c * sin_l)
        return jnp.concatenate(cosines + sines, 0)

    def tables(k):
        u = turn(k)
        off = recv_a[u, rows : 2 * rows, :]
        strip = (u * sub + part).astype(f32)
        pos = (jnp.where(upper, strip, tile_row) + off) / count
        cos_p, sin_p = cos_sin(0.5 * (pos + pltpu.roll(pos, tiles, 0)))
        phi[k, 0] = cos_p
        phi[k, 1] = sin_p
        for h in range(tiles):
            cols = slice(h * lanes, (h + 1) * lanes)
            tx = harmonics(jnp.broadcast_to(pos[h : h + 1], (8, lanes)))
            table_x[k, :, cols] = tx.astype(bf16)
            ty = harmonics(jnp.broadcast_to(pos[tiles + h : tiles + h + 1], (8, lanes)))
            table_y[k, :, cols] = ty.astype(bf16)
            wide_y[k, :, cols] = ty

    def project(k, density):
        rotated = density * phi[k, 0] + times_i(density) * phi[k, 1]
        twisted = []
        for h in range(tiles):
            cols = slice(h * lanes, (h + 1) * lanes)
            ty = table_y[k, :, cols]
            both = []
            for c in range(2):
                row = c * tiles + h
                q = jnp.broadcast_to(rotated[row : row + 1], (16, lanes)).astype(bf16)
                both.append(ty * jnp.concatenate([q] * (modes_y // 16), 0))
            twisted.append(jnp.concatenate(both, 0))
        return rows_dot(jnp.concatenate(twisted, 1), table_x[k])

    def weighted(total):
        x_r, y_r = total[0:half_y], total[half_y:modes_y]
        x_i, y_i = total[modes_y : modes_y + half_y], total[modes_y + half_y :]
        rx_r, ry_r, rx_i, ry_i = [pltpu.roll(x, half_x, 1) for x in (x_r, y_r, x_i, y_i)]
        f_0 = fact[0:half_y, 0:modes_x]
        f_s = fact[0:half_y, modes_x:]
        f_t = fact[half_y:, 0:modes_x]
        f_1 = fact[half_y:, modes_x:]
        return jnp.concatenate(
            [
                f_0 * x_r + f_1 * ry_r - f_s * rx_i + f_t * y_i,
                f_0 * y_r - f_1 * rx_r - f_t * x_i - f_s * ry_i,
                f_0 * x_i + f_1 * ry_i + f_s * rx_r - f_t * y_r,
                f_0 * y_i - f_1 * rx_i + f_t * x_r + f_s * ry_r,
            ],
            0,
        ).astype(bf16)

    def expand(k, matrix):
        for h in range(tiles):
            cols = slice(h * lanes, (h + 1) * lanes)
            summed = jnp.dot(matrix, table_x[k, :, cols], preferred_element_type=f32)
            ty = wide_y[k, :, cols]
            for c in range(2):
                row = c * tiles + h
                far[k, row : row + 1, :] = jnp.sum(
                    summed[c * modes_y : (c + 1) * modes_y] * ty, 0, keepdims=True
                )
        value = far[k]
        return value * phi[k, 0] - times_i(value) * phi[k, 1]

    def near_field(halo):
        result = []
        for h in range(tiles):
            picked = []
            for j in range(9):
                slot = neighbor[0, h, j]
                row = slot // 3
                column = lax.rem(w * tiles + h + lax.rem(slot, 3) - 1 + count_y, count_y)
                picked.append(halo[row, column])
            left = jnp.concatenate(picked, 1)
            right = jnp.concatenate(
                [
                    jnp.concatenate([kernel_vmem[h, j, c] for j in range(9)], 0)
                    for c in range(2)
                ],
                1,
            )
            product = jnp.dot(left, right, preferred_element_type=f32)
            result.append(
                (
                    product[:vectors, :lanes] - product[vectors:, lanes:],
                    product[:vectors, lanes:] + product[vectors:, :lanes],
                )
            )
        return result

    pl.semaphore_wait(barrier, greeted)
    copies_1 = halo_copies(0, halo_1)
    start(column_copy(phase_a, 0, send_a.at[turn(0)], recv_a))
    for copy in copies_1:
        start(copy)
    for k in range(1, vectors):
        start(column_copy(phase_a, k, send_a.at[turn(k)], recv_a))

    for load in loads[2:6]:
        load.wait()
    my_weight = weight_vmem[frequency[mine]] * (1.0 / math.sqrt(modes_x * modes_y * panels))
    diagonal = jnp.sum(jnp.sum(my_weight, 0, keepdims=True), 1, keepdims=True)
    exact = lax.Precision.HIGHEST

    def pick(lattice, half):
        index = lax.broadcasted_iota(jnp.int32, (half, 2 * half), 0)
        given = jnp.broadcast_to(lattice[...], index.shape)
        plus = jnp.where(given == index + half, 1.0, 0.0)
        minus = jnp.where(given == half - 1 - index, 1.0, 0.0)
        return plus + minus, plus - minus

    even_y, odd_y = pick(lattice_y, half_y)
    even_x, odd_x = pick(lattice_x, half_x)
    by_y = rows_dot(jnp.concatenate([even_y, odd_y], 0), my_weight, exact)
    pick_x = jnp.concatenate([even_x, even_x, -odd_x, odd_x], 0)
    fact[...] = rows_dot(by_y, pick_x, exact)

    column_wait(phase_a, 0, recv_a)
    tables(0)

    def send_tiles(pairs, slab):
        for h in range(tiles):
            for c in range(2):
                slab[:, c * tiles + h, :] = pairs[h][c]

    for load in loads[6:]:
        load.wait()
    for copy in copies_1:
        copy.wait_recv()
    send_tiles(near_field(halo_1), send_n)
    for k in range(vectors):
        start(column_copy(phase_n, k, send_n.at[turn(k)], recv_n))

    total = None
    for k in range(1, vectors):
        column_wait(phase_a, k, recv_a)
    for k in range(vectors):
        if k:
            tables(k)
        dense[k] = recv_a[turn(k), 0:rows, :].astype(bf16).astype(f32)
        term = project(k, dense[k])
        total = term if total is None else total + term

    def gather_sum(phase, source, target):
        if members == 2:
            return source[...] + target[lax.rem(member + 1, members)]
        target[member] = source[...]
        return jnp.sum(target[...], 0)

    send_g1[...] = total
    for k in range(1, members):
        start(mate_copy(0, k, send_g1, recv_g1))
    for k in range(1, members):
        mate_wait(0, k, recv_g1)
    matrix = weighted(gather_sum(0, send_g1, recv_g1))

    fields = [expand(k, matrix) for k in range(vectors)]
    for k in range(vectors):
        column_wait(phase_n, k, recv_n)

    def halo_message(k, before, own, after):
        rounded = jnp.concatenate([before, own, after, after], 0).astype(bf16)
        send_h[k] = rounded
        start(column_copy(phase_h, k, send_h.at[k], recv_h))
        inner = (row_id == 1) | (row_id == tiles + 1)
        edge = inner | (row_id == tiles - 2) | (row_id == 2 * tiles - 2)
        moved = jnp.where(inner, pltpu.roll(own, 1, 0), pltpu.roll(own, 2 * tiles - 1, 0))
        rounded = jnp.concatenate([jnp.where(edge, moved, before), after], 0).astype(bf16)
        if k:
            send_o[k] = rounded
            start(column_copy(phase_o, k, send_o.at[k], recv_o, w))
        else:
            recv_o[mine] = rounded

    total = None
    values = []
    zero = jnp.zeros((rows, lanes), f32)
    sums = [zero] * 5
    for k in range(vectors):
        u = turn(k)
        given = recv_a[u, 0:rows, :]
        base = dense[k]
        value = fields[k] + recv_n[u] - diagonal * base
        zeta[k] = value
        turned = times_i(value)
        terms = (given * given, base * base, base * value, -base * turned, value * value)
        sums = [x + y for x, y in zip(sums, terms)]
        values.append(value)
        if sub > 1:
            send_z[k] = value
            start(column_copy(phase_z, k, send_z.at[k], recv_z))
        elif k >= 2:
            halo_message(k - 1, *values[k - 2 : k + 1])
        term = project(k, value)
        total = term if total is None else total + term

    if sub == 1:
        halo_message(vectors - 1, values[-2], values[-1], values[0])
        halo_message(0, values[-1], values[0], values[1])
    send_g2[0 : 2 * modes_y] = total
    line = jnp.zeros((rows, lanes), f32)
    for number, x in enumerate(sums):
        whole = jnp.sum(jnp.sum(x, 0, keepdims=True), 1, keepdims=True)
        line = jnp.where(row_id == number, whole, line)
    send_g2[2 * modes_y :] = line
    for k in range(1, members):
        start(mate_copy(1, k, send_g2, recv_g2))

    if sub > 1:
        for k in range(vectors):
            column_wait(phase_z, k, recv_z)
        for h in range(tiles):
            halo_2[1, w * tiles + h] = jnp.concatenate(
                [recv_z[:, c * tiles + h, :].astype(bf16) for c in range(2)], 0
            )
        copies_2 = halo_copies(1, halo_2)
        for copy in copies_2:
            start(copy)

    for k in range(1, members):
        mate_wait(1, k, recv_g2)
    total = gather_sum(1, send_g2, recv_g2)
    matrix = weighted(total[0 : 2 * modes_y])
    line = total[2 * modes_y :]
    squares, base_sq, inner_r, inner_i, value_sq = [line[i : i + 1] for i in range(5)]
    shift = 0.5 + diagonal
    variance = squares / panels + eps_norm
    scale = jnp.sqrt(variance)
    over = 1.0 / (panels * variance)
    rest_r = (shift * base_sq + inner_r) * over
    coef_i = inner_i * over
    coef_r = rest_r
    move_r = coef_r - shift
    update_sq = (
        value_sq
        - 2.0 * (move_r * inner_r + coef_i * inner_i)
        + (move_r * move_r + coef_i * coef_i) * base_sq
    )
    update_scale = jnp.sqrt(jnp.maximum(update_sq, 0.0) * over + eps_norm)
    inverse = 1.0 / (scale * update_scale)
    result = jnp.zeros((rows, lanes), f32)
    for number, x in enumerate((scale, coef_r, coef_i, update_scale, inverse)):
        result = jnp.where(row_id == number, x, result)

    for k in range(vectors):
        u = turn(k)
        value = zeta[k]
        image = value + shift * dense[k]
        out = expand(k, matrix) + 0.5 * value - move_r * image - coef_i * times_i(image)
        send_f[u, 0:rows, :] = out * inverse
        send_f[u, rows : 2 * rows, :] = result
        start(column_copy(phase_f, k, send_f.at[turn(k)], recv_f))

    if sub > 1:
        for copy in copies_2:
            copy.wait_recv()
    else:
        for k in range(vectors):
            column_wait(phase_h, k, recv_h)
            if k:
                column_wait(phase_o, k, recv_o)
        near_h[...] = recv_h[...].astype(f32)
        near_o[...] = recv_o[...].astype(f32)
        for strip in range(3):
            for h in range(tiles):
                first = strip * rows + h
                pair = [near_h[:, first + c * tiles, :] for c in range(2)]
                halo_2[strip, w * tiles + h] = jnp.concatenate(pair, 0).astype(bf16)
            for h in (0, tiles - 1):
                first = (h, 1 if h == 0 else h - 1, rows + h)[strip]
                pair = [near_o[:, first + c * tiles, :] for c in range(2)]
                halo_2[strip, other_w * tiles + h] = jnp.concatenate(pair, 0).astype(bf16)
    near = near_field(halo_2)
    for k in range(vectors):
        column_wait(phase_f, k, recv_f)
    scaling = recv_f[:, rows + 4, :]
    for h in range(tiles):
        for c in range(2):
            image_out[h, c] = recv_f[:, c * tiles + h, :] + near[h][c] * scaling
    row = lax.broadcasted_iota(jnp.int32, (vectors, lanes), 0)
    lane = lax.broadcasted_iota(jnp.int32, (vectors, lanes), 1)
    for number in range(4):
        value = recv_f[:, rows + number, :]
        line = jnp.sum(jnp.where(row == lane, value, 0.0), 0, keepdims=True)
        arnoldi_out[number : number + 1, :] = line[:, :vectors]

    for copy in started:
        copy.wait_send()


def hand_over(image, arnoldi, image_out, arnoldi_out):
    image_out[...] = image[...]
    arnoldi_out[...] = arnoldi[...]


def per_device(
    size_t,
    size_w,
    residual,
    kernel,
    offsets,
    neighbor,
    frequency,
    lattice_x,
    lattice_y,
    spectral_weight,
):
    strips, tiles, _, vectors, lanes = residual.shape
    modes_x, modes_y = spectral_weight.shape[1:]
    assert strips == 1 and lanes == 128 and size_w == 2 and size_t > 2
    assert size_t % vectors == 0 and tiles == 4 and vectors == 8
    assert modes_x == 128 and modes_y == 128
    members = size_w * (size_t // vectors)
    rows = 2 * tiles
    vmem = pl.BlockSpec(memory_space=pltpu.VMEM)
    anywhere = pl.BlockSpec(memory_space=pl.ANY)
    halo = pltpu.VMEM((3, size_w * tiles, 2 * vectors, lanes), bf16)
    wide = pltpu.VMEM((vectors, 2 * rows, lanes), f32)
    slim = pltpu.VMEM((vectors, rows, lanes), f32)
    image, arnoldi = pl.pallas_call(
        functools.partial(body, size_t, size_w, tiles, vectors, modes_x, modes_y),
        out_shape=(
            pltpu.VMEM((tiles, 2, vectors, lanes), f32),
            pltpu.VMEM((4, vectors), f32),
        ),
        in_specs=[anywhere] * 8,
        out_specs=(vmem, vmem),
        scratch_shapes=[
            wide,
            wide,
            slim,
            slim,
            slim,
            slim,
            pltpu.VMEM((vectors, 4 * rows, lanes), bf16),
            pltpu.VMEM((vectors, 4 * rows, lanes), bf16),
            pltpu.VMEM((vectors, 2 * rows, lanes), bf16),
            pltpu.VMEM((vectors, 2 * rows, lanes), bf16),
            pltpu.VMEM((vectors, 4 * rows, lanes), f32),
            wide,
            wide,
            wide,
            pltpu.VMEM((2 * modes_y, modes_x), f32),
            pltpu.VMEM((members, 2 * modes_y, modes_x), f32),
            pltpu.VMEM((2 * modes_y + rows, modes_x), f32),
            pltpu.VMEM((members, 2 * modes_y + rows, modes_x), f32),
            halo,
            halo,
            pltpu.VMEM((vectors, modes_x, tiles * lanes), bf16),
            pltpu.VMEM((vectors, modes_y, tiles * lanes), bf16),
            pltpu.VMEM((vectors, modes_y, tiles * lanes), f32),
            pltpu.VMEM((vectors, 2, rows, lanes), f32),
            slim,
            slim,
            slim,
            pltpu.VMEM((modes_y, 2 * modes_x), f32),
            pltpu.VMEM(residual.shape[1:], f32),
            pltpu.VMEM(offsets.shape[1:], f32),
            pltpu.SMEM(neighbor.shape, jnp.int32),
            pltpu.SMEM(frequency.shape, jnp.int32),
            pltpu.VMEM((1, modes_x), jnp.int32),
            pltpu.VMEM((1, modes_y), jnp.int32),
            pltpu.VMEM((tiles, 9, 2, lanes, lanes), bf16),
            pltpu.VMEM(spectral_weight.shape, f32),
            pltpu.SemaphoreType.DMA((8,)),
            pltpu.SemaphoreType.DMA((6, vectors)),
            pltpu.SemaphoreType.DMA((6, vectors)),
            pltpu.SemaphoreType.DMA((2, members)),
            pltpu.SemaphoreType.DMA((2, members)),
            pltpu.SemaphoreType.DMA((2, 5)),
            pltpu.SemaphoreType.DMA((2, 5)),
        ],
        compiler_params=pltpu.CompilerParams(
            collective_id=0, has_side_effects=True, vmem_limit_bytes=56 * 1024 * 1024
        ),
        name="arnoldi_pair",
    )(
        residual[0],
        kernel[0],
        offsets[0],
        neighbor,
        frequency,
        lattice_x[None],
        lattice_y[None],
        spectral_weight,
    )
    image, arnoldi = [
        pltpu.with_memory_space_constraint(x, pltpu.VMEM) for x in (image, arnoldi)
    ]
    image, arnoldi = pl.pallas_call(
        hand_over,
        out_shape=(
            jax.ShapeDtypeStruct(image.shape, f32),
            jax.ShapeDtypeStruct(arnoldi.shape, f32),
        ),
        in_specs=[vmem, vmem],
        out_specs=(vmem, vmem),
        name="hand_over",
    )(image, arnoldi)
    return image[None], arnoldi


def solution(mesh):
    return jax.shard_map(
        functools.partial(per_device, mesh.shape["tile"], mesh.shape["wave"]),
        mesh=mesh,
        in_specs=(
            P(("grp", "tile"), "wave", None, None, None),
            P(("grp", "tile"), "wave", None, None, None, None),
            P(("grp", "tile"), "wave", None, None),
            P(("grp", "tile"), "wave", None),
            P("grp"),
            P(),
            P(),
            P(),
        ),
        out_specs=(P(("grp", "tile"), "wave", None, None, None), P("grp", None)),
        check_vma=False,
    )
```

```python
import functools
import math

import jax
import jax.numpy as jnp
from jax import lax
from jax.experimental import pallas as pl
from jax.experimental.pallas import tpu as pltpu
from jax.sharding import PartitionSpec as P

eps_norm = 1e-06
f32 = jnp.float32
bf16 = jnp.bfloat16
MESH = pl.DeviceIdType.MESH
phase_a, phase_n, phase_z, phase_f, phase_h, phase_o = range(6)

cos_poly = (
    0.9999992107823232,
    -19.73898035576408,
    64.9286574210355,
    -85.2716215343227,
    58.79049212023139,
    -21.071105627794083,
)
sin_poly = (
    6.283184916495429,
    -41.34158923268887,
    81.59994332979169,
    -76.61447253134614,
    41.34288235500671,
    -12.471243535733244,
)


def horner(coefs, z):
    total = coefs[-1] * z + coefs[-2]
    for c in coefs[-3::-1]:
        total = total * z + c
    return total


def cos_sin(turns):
    r = turns - jnp.round(turns)
    z = r * r
    return horner(cos_poly, z), r * horner(sin_poly, z)


def rows_dot(a, b, precision=None):
    return lax.dot_general(
        a, b, (((1,), (1,)), ((), ())), precision=precision, preferred_element_type=f32
    )


def body(
    size_t,
    size_w,
    tiles,
    vectors,
    modes_x,
    modes_y,
    residual_any,
    blocks,
    offsets_any,
    neighbor_any,
    frequency_any,
    lattice_x_any,
    lattice_y_any,
    weight,
    image_out,
    arnoldi_out,
    send_a,
    recv_a,
    send_n,
    recv_n,
    send_z,
    recv_z,
    send_h,
    recv_h,
    send_o,
    recv_o,
    near_h,
    near_o,
    send_f,
    recv_f,
    send_g1,
    recv_g1,
    send_g2,
    recv_g2,
    halo_1,
    halo_2,
    table_x,
    table_y,
    wide_y,
    phi,
    dense,
    zeta,
    far,
    fact,
    coeffs,
    halves,
    residual,
    offsets,
    neighbor,
    frequency,
    lattice_x,
    lattice_y,
    kernel_vmem,
    weight_vmem,
    load_sem,
    col_send,
    col_recv,
    mate_send,
    mate_recv,
    halo_send,
    halo_recv,
):
    devices = size_t * size_w
    sub = size_t // vectors
    members = size_w * sub
    rows = 2 * tiles
    half_x = modes_x // 2
    half_y = modes_y // 2
    lanes = 128
    panels = devices * tiles * lanes
    count_x = size_t
    count_y = size_w * tiles
    t = lax.axis_index("tile")
    w = lax.axis_index("wave")
    me = t * size_w + w
    mine = t // sub
    part = lax.rem(t, sub)
    member = part * size_w + w

    up = lax.rem(t + 1, size_t)
    down = lax.rem(t + size_t - 1, size_t)
    other_w = lax.rem(w + 1, size_w)

    barrier = pltpu.get_barrier_semaphore()

    def greet(to_t, to_w):
        place = {"tile": to_t, "wave": to_w}
        pl.semaphore_signal(barrier, inc=1, device_id=place, device_id_type=MESH)

    if sub == 1:
        greeted = vectors + 2
        greet(up, w)
        greet(down, w)
        for k in range(vectors):
            greet(lax.rem(t + k, size_t), other_w)
    else:
        greeted = devices - 1

        def greet_one(k, carry):
            other = lax.rem(me + k, devices)
            greet(other // size_w, lax.rem(other, size_w))
            return carry

        lax.fori_loop(1, devices, greet_one, 0)

    loads = []
    for number, (source, target) in enumerate(
        (
            (residual_any, residual),
            (offsets_any, offsets),
            (frequency_any, frequency),
            (weight, weight_vmem),
            (lattice_x_any, lattice_x),
            (lattice_y_any, lattice_y),
            (neighbor_any, neighbor),
            (blocks, kernel_vmem),
        )
    ):
        loads.append(pltpu.make_async_copy(source, target, load_sem.at[number]))
        loads[-1].start()

    bits = [lax.rem(mine // (1 << i), 2) for i in range(3)]

    def turn(k):
        return sum(((1 - b) if (k >> i) & 1 else b) * (1 << i) for i, b in enumerate(bits))

    def column_copy(phase, k, source, target, wave=None):
        return pltpu.make_async_remote_copy(
            src_ref=source,
            dst_ref=target.at[mine],
            send_sem=col_send.at[phase, k],
            recv_sem=col_recv.at[phase, k],
            device_id={"tile": turn(k) * sub + part, "wave": other_w if wave is None else wave},
            device_id_type=MESH,
        )

    def column_wait(phase, k, target):
        slot = target.at[turn(k)]
        pltpu.make_async_copy(slot, slot, col_recv.at[phase, k]).wait()

    def mate_copy(phase, k, source, target):
        other = lax.rem(member + k, members)
        return pltpu.make_async_remote_copy(
            src_ref=source,
            dst_ref=target.at[member],
            send_sem=mate_send.at[phase, k],
            recv_sem=mate_recv.at[phase, members - k],
            device_id={"tile": mine * sub + other // size_w, "wave": lax.rem(other, size_w)},
            device_id_type=MESH,
        )

    def mate_wait(phase, k, target):
        slot = target.at[lax.rem(member + k, members)]
        pltpu.make_async_copy(slot, slot, mate_recv.at[phase, k]).wait()

    def halo_copies(phase, halo):
        copies = []
        targets = ((up, w, 0), (up, other_w, 0), (t, other_w, 1), (down, w, 2), (down, other_w, 2))
        for number, (to_t, to_w, row) in enumerate(targets):
            copies.append(
                pltpu.make_async_remote_copy(
                    src_ref=halo.at[1, pl.ds(w * tiles, tiles)],
                    dst_ref=halo.at[row, pl.ds(w * tiles, tiles)],
                    send_sem=halo_send.at[phase, number],
                    recv_sem=halo_recv.at[phase, number],
                    device_id={"tile": to_t, "wave": to_w},
                    device_id_type=MESH,
                )
            )
        return copies

    started = []

    def start(copy):
        copy.start()
        started.append(copy)

    row_id = lax.broadcasted_iota(jnp.int32, (rows, lanes), 0)
    upper = row_id < tiles
    sign = jnp.where(upper, -1.0, 1.0)

    def times_i(x):
        return pltpu.roll(x, tiles, 0) * sign

    if sub == 1:
        for strip in range(3):
            for h in range(1, tiles - 1):
                halo_2[strip, other_w * tiles + h] = jnp.zeros((2 * vectors, lanes), bf16)
    loads[0].wait()
    loads[1].wait()
    offset_rows = jnp.concatenate([offsets[:, 0, :], offsets[:, 1, :]], 0)
    for h in range(tiles):
        rounded = []
        for c in range(2):
            value = residual[h, c]
            send_a[:, c * tiles + h, :] = value
            rounded.append(value.astype(bf16))
        halo_1[1, w * tiles + h] = jnp.concatenate(rounded, 0)
    for v in range(vectors):
        send_a[v, rows : 2 * rows, :] = offset_rows

    low = lax.broadcasted_iota(jnp.int32, (8, lanes), 0).astype(f32) + 0.5
    count = jnp.where(upper, float(count_x), float(count_y))
    tile_row = (row_id - tiles + other_w * tiles).astype(f32)

    def harmonics(position, cos_8, sin_8):
        cos_b, sin_b = cos_sin(position * low)
        cosines = [cos_b, cos_b * cos_8 - sin_b * sin_8]
        sines = [sin_b, sin_b * cos_8 + cos_b * sin_8]
        twice = cos_8 + cos_8
        for series in (cosines, sines):
            for m in range(2, 8):
                series.append(twice * series[-1] - series[-2])
        return jnp.concatenate(cosines + sines, 0)

    def tables(k):
        u = turn(k)
        off = recv_a[u, rows : 2 * rows, :]
        strip = (u * sub + part).astype(f32)
        pos = (jnp.where(upper, strip, tile_row) + off) / count
        cos_p, sin_p = cos_sin(0.5 * (pos + pltpu.roll(pos, tiles, 0)))
        cos_8, sin_8 = cos_sin(8.0 * pos)
        phi[k, 0] = cos_p
        phi[k, 1] = sin_p
        given = []
        for h in range(tiles):
            tx = harmonics(*[jnp.broadcast_to(x[h : h + 1], (8, lanes)) for x in (pos, cos_8, sin_8)])
            table_x[k, h] = tx.astype(bf16)
            row = tiles + h
            ty = harmonics(
                *[jnp.broadcast_to(x[row : row + 1], (8, lanes)) for x in (pos, cos_8, sin_8)]
            )
            table_y[k, h] = ty.astype(bf16)
            wide_y[k, h] = ty
            given.append(ty.astype(bf16))
        return given

    def add(totals, terms):
        return terms if totals is None else [x + y for x, y in zip(totals, terms)]

    def project(k, density, given=None):
        rotated = density * phi[k, 0] + times_i(density) * phi[k, 1]
        twisted = []
        for h in range(tiles):
            ty = table_y[k, h] if given is None else given[h]
            both = []
            for c in range(2):
                row = c * tiles + h
                q = jnp.broadcast_to(rotated[row : row + 1], (16, lanes)).astype(bf16)
                both.append(ty * jnp.concatenate([q] * (modes_y // 16), 0))
            twisted.append(jnp.concatenate(both, 0))
        return [
            rows_dot(
                jnp.concatenate(twisted[h : h + 2], 1),
                jnp.concatenate([table_x[k, h], table_x[k, h + 1]], 1),
            )
            for h in range(0, tiles, 2)
        ]

    def both_sums(totals):
        halves[w] = totals[0]
        halves[other_w] = totals[1]
        return halves[0] + halves[1]

    def weigh(total):
        x_r, y_r = total[0:half_y], total[half_y:modes_y]
        x_i, y_i = total[modes_y : modes_y + half_y], total[modes_y + half_y :]
        rx_r, ry_r, rx_i, ry_i = [pltpu.roll(x, half_x, 1) for x in (x_r, y_r, x_i, y_i)]
        f_0 = fact[0:half_y, 0:modes_x]
        f_s = fact[0:half_y, modes_x:]
        f_t = fact[half_y:, 0:modes_x]
        f_1 = fact[half_y:, modes_x:]
        matrix = jnp.concatenate(
            [
                f_0 * x_r + f_1 * ry_r - f_s * rx_i + f_t * y_i,
                f_0 * y_r - f_1 * rx_r - f_t * x_i - f_s * ry_i,
                f_0 * x_i + f_1 * ry_i + f_s * rx_r - f_t * y_r,
                f_0 * y_i - f_1 * rx_i + f_t * x_r + f_s * ry_r,
            ],
            0,
        ).astype(bf16)
        coeffs[w] = matrix
        coeffs[other_w] = matrix

    def expand(k):
        for h in range(0, tiles, 2):
            summed = jnp.dot(
                coeffs[(w, other_w)[h // 2]],
                jnp.concatenate([table_x[k, h], table_x[k, h + 1]], 1),
                preferred_element_type=f32,
            )
            for side in range(2):
                cols = slice(side * lanes, (side + 1) * lanes)
                ty = wide_y[k, h + side]
                for c in range(2):
                    row = c * tiles + h + side
                    far[k, row : row + 1, :] = jnp.sum(
                        summed[c * modes_y : (c + 1) * modes_y, cols] * ty, 0, keepdims=True
                    )
        value = far[k]
        return value * phi[k, 0] - times_i(value) * phi[k, 1]

    def near_field(halo):
        result = []
        for h in range(tiles):
            picked = []
            for j in range(9):
                slot = neighbor[0, h, j]
                row = slot // 3
                column = lax.rem(w * tiles + h + lax.rem(slot, 3) - 1 + count_y, count_y)
                picked.append(halo[row, column])
            left = jnp.concatenate(picked, 1)
            right = jnp.concatenate(
                [
                    jnp.concatenate([kernel_vmem[h, j, c] for j in range(9)], 0)
                    for c in range(2)
                ],
                1,
            )
            product = jnp.dot(left, right, preferred_element_type=f32)
            result.append(
                (
                    product[:vectors, :lanes] - product[vectors:, lanes:],
                    product[:vectors, lanes:] + product[vectors:, :lanes],
                )
            )
        return result

    pl.semaphore_wait(barrier, greeted)
    copies_1 = halo_copies(0, halo_1)
    for copy in copies_1:
        start(copy)
    for k in reversed(range(vectors)):
        start(column_copy(phase_a, k, send_a.at[turn(k)], recv_a))

    for load in loads[2:6]:
        load.wait()
    my_weight = weight_vmem[frequency[mine]] * (1.0 / math.sqrt(modes_x * modes_y * panels))
    diagonal = jnp.sum(jnp.sum(my_weight, 0, keepdims=True), 1, keepdims=True)
    exact = lax.Precision.HIGHEST

    def pick(lattice, half):
        index = lax.broadcasted_iota(jnp.int32, (half, 2 * half), 0)
        given = jnp.broadcast_to(lattice[...], index.shape)
        plus = jnp.where(given == index + half, 1.0, 0.0)
        minus = jnp.where(given == half - 1 - index, 1.0, 0.0)
        return plus + minus, plus - minus

    even_y, odd_y = pick(lattice_y, half_y)
    even_x, odd_x = pick(lattice_x, half_x)
    by_y = rows_dot(jnp.concatenate([even_y, odd_y], 0), my_weight, exact)
    pick_x = jnp.concatenate([even_x, even_x, -odd_x, odd_x], 0)
    fact[...] = rows_dot(by_y, pick_x, exact)

    column_wait(phase_a, 0, recv_a)
    tables(0)

    def send_tiles(pairs, slab):
        for h in range(tiles):
            for c in range(2):
                slab[:, c * tiles + h, :] = pairs[h][c]

    for load in loads[6:]:
        load.wait()
    for copy in copies_1:
        copy.wait_recv()
    send_tiles(near_field(halo_1), send_n)
    for k in reversed(range(vectors)):
        start(column_copy(phase_n, k, send_n.at[turn(k)], recv_n))

    total = None
    for k in range(vectors):
        given = None
        if k:
            column_wait(phase_a, k, recv_a)
            given = tables(k)
        dense[k] = recv_a[turn(k), 0:rows, :].astype(bf16).astype(f32)
        total = add(total, project(k, dense[k], given))

    def gather_sum(phase, source, target):
        if members == 2:
            return source[...] + target[lax.rem(member + 1, members)]
        target[member] = source[...]
        return jnp.sum(target[...], 0)

    send_g1[...] = both_sums(total)
    for k in range(1, members):
        start(mate_copy(0, k, send_g1, recv_g1))
    for k in range(1, members):
        mate_wait(0, k, recv_g1)
    weigh(gather_sum(0, send_g1, recv_g1))

    fields = [expand(k) for k in range(vectors)]
    for k in range(vectors):
        column_wait(phase_n, k, recv_n)

    def halo_message(k):
        u = turn(k)
        before = zeta[lax.rem(u + vectors - 1, vectors)]
        own = zeta[u]
        after = zeta[lax.rem(u + 1, vectors)]
        rounded = jnp.concatenate([before, own, after, after], 0).astype(bf16)
        send_h[k] = rounded
        start(column_copy(phase_h, k, send_h.at[k], recv_h))
        inner = (row_id == 1) | (row_id == tiles + 1)
        edge = inner | (row_id == tiles - 2) | (row_id == 2 * tiles - 2)
        moved = jnp.where(inner, pltpu.roll(own, 1, 0), pltpu.roll(own, 2 * tiles - 1, 0))
        rounded = jnp.concatenate([jnp.where(edge, moved, before), after], 0).astype(bf16)
        if k:
            send_o[k] = rounded
            start(column_copy(phase_o, k, send_o.at[k], recv_o, w))
        else:
            recv_o[mine] = rounded

    zero = jnp.zeros((rows, lanes), f32)
    sums = [zero] * 5
    values = []
    for k in range(vectors):
        u = turn(k)
        given = recv_a[u, 0:rows, :]
        base = dense[k]
        value = fields[k] + recv_n[u] - diagonal * base
        values.append(value)
        zeta[u] = value
        turned = times_i(value)
        terms = (given * given, base * base, base * value, -base * turned, value * value)
        sums = [x + y for x, y in zip(sums, terms)]
        if sub > 1:
            send_z[k] = value
            start(column_copy(phase_z, k, send_z.at[k], recv_z))

    total = None
    for k in reversed(range(vectors)):
        if sub == 1:
            halo_message(k)
        total = add(total, project(k, values[k]))
    send_g2[0 : 2 * modes_y] = both_sums(total)
    line = jnp.zeros((rows, lanes), f32)
    for number, x in enumerate(sums):
        whole = jnp.sum(jnp.sum(x, 0, keepdims=True), 1, keepdims=True)
        line = jnp.where(row_id == number, whole, line)
    send_g2[2 * modes_y :] = line
    for k in range(1, members):
        start(mate_copy(1, k, send_g2, recv_g2))

    if sub > 1:
        for k in range(vectors):
            column_wait(phase_z, k, recv_z)
        for h in range(tiles):
            halo_2[1, w * tiles + h] = jnp.concatenate(
                [recv_z[:, c * tiles + h, :].astype(bf16) for c in range(2)], 0
            )
        copies_2 = halo_copies(1, halo_2)
        for copy in copies_2:
            start(copy)

    for k in range(1, members):
        mate_wait(1, k, recv_g2)
    total = gather_sum(1, send_g2, recv_g2)
    weigh(total[0 : 2 * modes_y])
    line = total[2 * modes_y :]
    squares, base_sq, inner_r, inner_i, value_sq = [line[i : i + 1] for i in range(5)]
    shift = 0.5 + diagonal
    variance = squares / panels + eps_norm
    scale = jnp.sqrt(variance)
    over = 1.0 / (panels * variance)
    rest_r = (shift * base_sq + inner_r) * over
    coef_i = inner_i * over
    coef_r = rest_r
    move_r = coef_r - shift
    update_sq = (
        value_sq
        - 2.0 * (move_r * inner_r + coef_i * inner_i)
        + (move_r * move_r + coef_i * coef_i) * base_sq
    )
    update_scale = jnp.sqrt(jnp.maximum(update_sq, 0.0) * over + eps_norm)
    inverse = 1.0 / (scale * update_scale)
    result = jnp.zeros((rows, lanes), f32)
    for number, x in enumerate((scale, coef_r, coef_i, update_scale, inverse)):
        result = jnp.where(row_id == number, x, result)

    order = list(reversed(range(vectors)))
    field = expand(order[0])
    for number, k in enumerate(order):
        u = turn(k)
        coming = expand(order[number + 1]) if number + 1 < vectors else None
        value = zeta[u]
        image = value + shift * dense[k]
        out = field + 0.5 * value - move_r * image - coef_i * times_i(image)
        send_f[u, 0:rows, :] = out * inverse
        send_f[u, rows : 2 * rows, :] = result
        start(column_copy(phase_f, k, send_f.at[u], recv_f))
        field = coming

    last = started[-vectors:]
    for copy in started[:-vectors]:
        copy.wait_send()
    if sub > 1:
        for copy in copies_2:
            copy.wait_recv()
    else:
        for k in range(vectors):
            column_wait(phase_h, k, recv_h)
            if k:
                column_wait(phase_o, k, recv_o)
        near_h[...] = recv_h[...].astype(f32)
        near_o[...] = recv_o[...].astype(f32)
        for strip in range(3):
            for h in range(tiles):
                first = strip * rows + h
                pair = [near_h[:, first + c * tiles, :] for c in range(2)]
                halo_2[strip, w * tiles + h] = jnp.concatenate(pair, 0).astype(bf16)
            for h in (0, tiles - 1):
                first = (h, 1 if h == 0 else h - 1, rows + h)[strip]
                pair = [near_o[:, first + c * tiles, :] for c in range(2)]
                halo_2[strip, other_w * tiles + h] = jnp.concatenate(pair, 0).astype(bf16)
    near = near_field(halo_2)
    for k in range(vectors):
        column_wait(phase_f, k, recv_f)
    scaling = recv_f[:, rows + 4, :]
    for h in range(tiles):
        for c in range(2):
            image_out[h, c] = recv_f[:, c * tiles + h, :] + near[h][c] * scaling
    row = lax.broadcasted_iota(jnp.int32, (vectors, lanes), 0)
    lane = lax.broadcasted_iota(jnp.int32, (vectors, lanes), 1)
    for number in range(4):
        value = recv_f[:, rows + number, :]
        line = jnp.sum(jnp.where(row == lane, value, 0.0), 0, keepdims=True)
        arnoldi_out[number : number + 1, :] = line[:, :vectors]

    for copy in last:
        copy.wait_send()


def hand_over(image, arnoldi, image_out, arnoldi_out):
    image_out[...] = image[...]
    arnoldi_out[...] = arnoldi[...]


def per_device(
    size_t,
    size_w,
    residual,
    kernel,
    offsets,
    neighbor,
    frequency,
    lattice_x,
    lattice_y,
    spectral_weight,
):
    strips, tiles, _, vectors, lanes = residual.shape
    modes_x, modes_y = spectral_weight.shape[1:]
    assert strips == 1 and lanes == 128 and size_w == 2 and size_t > 2
    assert size_t % vectors == 0 and tiles == 4 and vectors == 8
    assert modes_x == 128 and modes_y == 128
    members = size_w * (size_t // vectors)
    rows = 2 * tiles
    vmem = pl.BlockSpec(memory_space=pltpu.VMEM)
    anywhere = pl.BlockSpec(memory_space=pl.ANY)
    halo = pltpu.VMEM((3, size_w * tiles, 2 * vectors, lanes), bf16)
    wide = pltpu.VMEM((vectors, 2 * rows, lanes), f32)
    slim = pltpu.VMEM((vectors, rows, lanes), f32)
    image, arnoldi = pl.pallas_call(
        functools.partial(body, size_t, size_w, tiles, vectors, modes_x, modes_y),
        out_shape=(
            pltpu.VMEM((tiles, 2, vectors, lanes), f32),
            pltpu.VMEM((4, vectors), f32),
        ),
        in_specs=[anywhere] * 8,
        out_specs=(vmem, vmem),
        scratch_shapes=[
            wide,
            wide,
            slim,
            slim,
            slim,
            slim,
            pltpu.VMEM((vectors, 4 * rows, lanes), bf16),
            pltpu.VMEM((vectors, 4 * rows, lanes), bf16),
            pltpu.VMEM((vectors, 2 * rows, lanes), bf16),
            pltpu.VMEM((vectors, 2 * rows, lanes), bf16),
            pltpu.VMEM((vectors, 4 * rows, lanes), f32),
            wide,
            wide,
            wide,
            pltpu.VMEM((2 * modes_y, modes_x), f32),
            pltpu.VMEM((members, 2 * modes_y, modes_x), f32),
            pltpu.VMEM((2 * modes_y + rows, modes_x), f32),
            pltpu.VMEM((members, 2 * modes_y + rows, modes_x), f32),
            halo,
            halo,
            pltpu.VMEM((vectors, tiles, modes_x, lanes), bf16),
            pltpu.VMEM((vectors, tiles, modes_y, lanes), bf16),
            pltpu.VMEM((vectors, tiles, modes_y, lanes), f32),
            pltpu.VMEM((vectors, 2, rows, lanes), f32),
            slim,
            slim,
            slim,
            pltpu.VMEM((modes_y, 2 * modes_x), f32),
            pltpu.VMEM((2, 2 * modes_y, modes_x), bf16),
            pltpu.VMEM((2, 2 * modes_y, modes_x), f32),
            pltpu.VMEM(residual.shape[1:], f32),
            pltpu.VMEM(offsets.shape[1:], f32),
            pltpu.SMEM(neighbor.shape, jnp.int32),
            pltpu.SMEM(frequency.shape, jnp.int32),
            pltpu.VMEM((1, modes_x), jnp.int32),
            pltpu.VMEM((1, modes_y), jnp.int32),
            pltpu.VMEM((tiles, 9, 2, lanes, lanes), bf16),
            pltpu.VMEM(spectral_weight.shape, f32),
            pltpu.SemaphoreType.DMA((8,)),
            pltpu.SemaphoreType.DMA((6, vectors)),
            pltpu.SemaphoreType.DMA((6, vectors)),
            pltpu.SemaphoreType.DMA((2, members)),
            pltpu.SemaphoreType.DMA((2, members)),
            pltpu.SemaphoreType.DMA((2, 5)),
            pltpu.SemaphoreType.DMA((2, 5)),
        ],
        compiler_params=pltpu.CompilerParams(
            collective_id=0, has_side_effects=True, vmem_limit_bytes=56 * 1024 * 1024
        ),
        name="arnoldi_pair",
    )(
        residual[0],
        kernel[0],
        offsets[0],
        neighbor,
        frequency,
        lattice_x[None],
        lattice_y[None],
        spectral_weight,
    )
    image, arnoldi = [
        pltpu.with_memory_space_constraint(x, pltpu.VMEM) for x in (image, arnoldi)
    ]
    image, arnoldi = pl.pallas_call(
        hand_over,
        out_shape=(
            jax.ShapeDtypeStruct(image.shape, f32),
            jax.ShapeDtypeStruct(arnoldi.shape, f32),
        ),
        in_specs=[vmem, vmem],
        out_specs=(vmem, vmem),
        name="hand_over",
    )(image, arnoldi)
    return image[None], arnoldi


def solution(mesh):
    return jax.shard_map(
        functools.partial(per_device, mesh.shape["tile"], mesh.shape["wave"]),
        mesh=mesh,
        in_specs=(
            P(("grp", "tile"), "wave", None, None, None),
            P(("grp", "tile"), "wave", None, None, None, None),
            P(("grp", "tile"), "wave", None, None),
            P(("grp", "tile"), "wave", None),
            P("grp"),
            P(),
            P(),
            P(),
        ),
        out_specs=(P(("grp", "tile"), "wave", None, None, None), P("grp", None)),
        check_vma=False,
    )
```

```python
import functools
import math

import jax
import jax.numpy as jnp
from jax import lax
from jax.experimental import pallas as pl
from jax.experimental.pallas import tpu as pltpu
from jax.sharding import PartitionSpec as P

eps_norm = 1e-06
f32 = jnp.float32
bf16 = jnp.bfloat16
MESH = pl.DeviceIdType.MESH
phase_a, phase_n, phase_z, phase_f, phase_h, phase_o = range(6)

cos_poly = (
    0.9999992107823232,
    -19.73898035576408,
    64.9286574210355,
    -85.2716215343227,
    58.79049212023139,
    -21.071105627794083,
)
sin_poly = (
    6.283184916495429,
    -41.34158923268887,
    81.59994332979169,
    -76.61447253134614,
    41.34288235500671,
    -12.471243535733244,
)


def horner(coefs, z):
    total = coefs[-1] * z + coefs[-2]
    for c in coefs[-3::-1]:
        total = total * z + c
    return total


def cos_sin(turns):
    r = turns - jnp.round(turns)
    z = r * r
    return horner(cos_poly, z), r * horner(sin_poly, z)


def rows_dot(a, b, precision=None):
    return lax.dot_general(
        a, b, (((1,), (1,)), ((), ())), precision=precision, preferred_element_type=f32
    )


def body(
    size_t,
    size_w,
    tiles,
    vectors,
    modes_x,
    modes_y,
    residual_any,
    blocks,
    offsets_any,
    neighbor_any,
    frequency_any,
    lattice_x_any,
    lattice_y_any,
    weight,
    image_out,
    arnoldi_out,
    send_a,
    recv_a,
    send_n,
    recv_n,
    send_z,
    recv_z,
    send_h,
    recv_h,
    send_o,
    recv_o,
    near_h,
    near_o,
    send_f,
    recv_f,
    send_g1,
    recv_g1,
    send_g2,
    recv_g2,
    halo_1,
    halo_2,
    edge_1,
    edge_2,
    table_x,
    table_y,
    wide_y,
    phi,
    dense,
    zeta,
    far,
    fact,
    coeffs,
    halves,
    residual,
    offsets,
    neighbor,
    frequency,
    lattice_x,
    lattice_y,
    kernel_vmem,
    weight_vmem,
    load_sem,
    col_send,
    col_recv,
    mate_send,
    mate_recv,
    halo_send,
    halo_recv,
):
    devices = size_t * size_w
    sub = size_t // vectors
    members = size_w * sub
    rows = 2 * tiles
    half_x = modes_x // 2
    half_y = modes_y // 2
    lanes = 128
    panels = devices * tiles * lanes
    count_x = size_t
    count_y = size_w * tiles
    t = lax.axis_index("tile")
    w = lax.axis_index("wave")
    me = t * size_w + w
    mine = t // sub
    part = lax.rem(t, sub)
    member = part * size_w + w

    up = lax.rem(t + 1, size_t)
    down = lax.rem(t + size_t - 1, size_t)
    other_w = lax.rem(w + 1, size_w)

    barrier = pltpu.get_barrier_semaphore()

    def greet(to_t, to_w):
        place = {"tile": to_t, "wave": to_w}
        pl.semaphore_signal(barrier, inc=1, device_id=place, device_id_type=MESH)

    if sub == 1:
        greeted = vectors + 2
        greet(up, w)
        greet(down, w)
        for k in range(vectors):
            greet(lax.rem(t + k, size_t), other_w)
    else:
        greeted = devices - 1

        def greet_one(k, carry):
            other = lax.rem(me + k, devices)
            greet(other // size_w, lax.rem(other, size_w))
            return carry

        lax.fori_loop(1, devices, greet_one, 0)

    loads = []
    for number, (source, target) in enumerate(
        (
            (residual_any, residual),
            (offsets_any, offsets),
            (frequency_any, frequency),
            (weight, weight_vmem),
            (lattice_x_any, lattice_x),
            (lattice_y_any, lattice_y),
            (neighbor_any, neighbor),
            (blocks, kernel_vmem),
        )
    ):
        loads.append(pltpu.make_async_copy(source, target, load_sem.at[number]))
        loads[-1].start()

    bits = [lax.rem(mine // (1 << i), 2) for i in range(3)]

    def turn(k):
        return sum(((1 - b) if (k >> i) & 1 else b) * (1 << i) for i, b in enumerate(bits))

    def column_copy(phase, k, source, target, wave=None):
        return pltpu.make_async_remote_copy(
            src_ref=source,
            dst_ref=target.at[mine],
            send_sem=col_send.at[phase, k],
            recv_sem=col_recv.at[phase, k],
            device_id={"tile": turn(k) * sub + part, "wave": other_w if wave is None else wave},
            device_id_type=MESH,
        )

    def column_wait(phase, k, target):
        slot = target.at[turn(k)]
        pltpu.make_async_copy(slot, slot, col_recv.at[phase, k]).wait()

    def mate_copy(phase, k, source, target):
        other = lax.rem(member + k, members)
        return pltpu.make_async_remote_copy(
            src_ref=source,
            dst_ref=target.at[member],
            send_sem=mate_send.at[phase, k],
            recv_sem=mate_recv.at[phase, members - k],
            device_id={"tile": mine * sub + other // size_w, "wave": lax.rem(other, size_w)},
            device_id_type=MESH,
        )

    def mate_wait(phase, k, target):
        slot = target.at[lax.rem(member + k, members)]
        pltpu.make_async_copy(slot, slot, mate_recv.at[phase, k]).wait()

    def halo_copies(phase, halo, edge):
        copies = []
        targets = ((down, w, 2), (down, other_w, 2), (up, w, 0), (up, other_w, 0), (t, other_w, 1))
        for number, (to_t, to_w, row) in enumerate(targets):
            own = number in (0, 2)
            copies.append(
                pltpu.make_async_remote_copy(
                    src_ref=halo.at[1, pl.ds(0, tiles)] if own else edge,
                    dst_ref=halo.at[row, pl.ds(0, tiles) if own else pl.ds(tiles, 2)],
                    send_sem=halo_send.at[phase, number],
                    recv_sem=halo_recv.at[phase, number],
                    device_id={"tile": to_t, "wave": to_w},
                    device_id_type=MESH,
                )
            )
        return copies

    def put_halo(h, value, halo, edge):
        halo[1, h] = value
        if h in (0, tiles - 1):
            edge[h // (tiles - 1)] = value

    started = []

    def start(copy):
        copy.start()
        started.append(copy)

    row_id = lax.broadcasted_iota(jnp.int32, (rows, lanes), 0)
    upper = row_id < tiles
    sign = jnp.where(upper, -1.0, 1.0)

    def times_i(x):
        return pltpu.roll(x, tiles, 0) * sign

    loads[0].wait()
    loads[1].wait()
    offset_rows = jnp.concatenate([offsets[:, 0, :], offsets[:, 1, :]], 0)
    for h in range(tiles):
        rounded = []
        for c in range(2):
            value = residual[h, c]
            send_a[:, c * tiles + h, :] = value
            rounded.append(value.astype(bf16))
        put_halo(h, jnp.concatenate(rounded, 0), halo_1, edge_1)
    for v in range(vectors):
        send_a[v, rows : 2 * rows, :] = offset_rows

    low = lax.broadcasted_iota(jnp.int32, (8, lanes), 0).astype(f32) + 0.5
    count = jnp.where(upper, float(count_x), float(count_y))
    tile_row = (row_id - tiles + other_w * tiles).astype(f32)

    def harmonics(position, cos_8, sin_8):
        cos_b, sin_b = cos_sin(position * low)
        cosines = [cos_b, cos_b * cos_8 - sin_b * sin_8]
        sines = [sin_b, sin_b * cos_8 + cos_b * sin_8]
        twice = cos_8 + cos_8
        for series in (cosines, sines):
            for m in range(2, 8):
                series.append(twice * series[-1] - series[-2])
        return jnp.concatenate(cosines + sines, 0)

    def tables(k):
        u = turn(k)
        off = recv_a[u, rows : 2 * rows, :]
        strip = (u * sub + part).astype(f32)
        pos = (jnp.where(upper, strip, tile_row) + off) / count
        cos_p, sin_p = cos_sin(0.5 * (pos + pltpu.roll(pos, tiles, 0)))
        cos_8, sin_8 = cos_sin(8.0 * pos)
        phi[k, 0] = cos_p
        phi[k, 1] = sin_p
        given = []
        for h in range(tiles):
            tx = harmonics(*[jnp.broadcast_to(x[h : h + 1], (8, lanes)) for x in (pos, cos_8, sin_8)])
            table_x[k, h] = tx.astype(bf16)
            row = tiles + h
            ty = harmonics(
                *[jnp.broadcast_to(x[row : row + 1], (8, lanes)) for x in (pos, cos_8, sin_8)]
            )
            table_y[k, h] = ty.astype(bf16)
            wide_y[k, h] = ty
            given.append(ty.astype(bf16))
        return given

    def add(totals, terms):
        return terms if totals is None else [x + y for x, y in zip(totals, terms)]

    def project(k, density, given=None):
        rotated = density * phi[k, 0] + times_i(density) * phi[k, 1]
        twisted = []
        for h in range(tiles):
            ty = table_y[k, h] if given is None else given[h]
            both = []
            for c in range(2):
                row = c * tiles + h
                q = jnp.broadcast_to(rotated[row : row + 1], (16, lanes)).astype(bf16)
                both.append(ty * jnp.concatenate([q] * (modes_y // 16), 0))
            twisted.append(jnp.concatenate(both, 0))
        return [
            rows_dot(
                jnp.concatenate(twisted[h : h + 2], 1),
                jnp.concatenate([table_x[k, h], table_x[k, h + 1]], 1),
            )
            for h in range(0, tiles, 2)
        ]

    def both_sums(totals):
        halves[w] = totals[0]
        halves[other_w] = totals[1]
        return halves[0] + halves[1]

    def weigh(total):
        x_r, y_r = total[0:half_y], total[half_y:modes_y]
        x_i, y_i = total[modes_y : modes_y + half_y], total[modes_y + half_y :]
        rx_r, ry_r, rx_i, ry_i = [pltpu.roll(x, half_x, 1) for x in (x_r, y_r, x_i, y_i)]
        f_0 = fact[0:half_y, 0:modes_x]
        f_s = fact[0:half_y, modes_x:]
        f_t = fact[half_y:, 0:modes_x]
        f_1 = fact[half_y:, modes_x:]
        matrix = jnp.concatenate(
            [
                f_0 * x_r + f_1 * ry_r - f_s * rx_i + f_t * y_i,
                f_0 * y_r - f_1 * rx_r - f_t * x_i - f_s * ry_i,
                f_0 * x_i + f_1 * ry_i + f_s * rx_r - f_t * y_r,
                f_0 * y_i - f_1 * rx_i + f_t * x_r + f_s * ry_r,
            ],
            0,
        ).astype(bf16)
        coeffs[w] = matrix
        coeffs[other_w] = matrix

    def expand(k):
        for h in range(0, tiles, 2):
            summed = jnp.dot(
                coeffs[(w, other_w)[h // 2]],
                jnp.concatenate([table_x[k, h], table_x[k, h + 1]], 1),
                preferred_element_type=f32,
            )
            for side in range(2):
                cols = slice(side * lanes, (side + 1) * lanes)
                ty = wide_y[k, h + side]
                for c in range(2):
                    row = c * tiles + h + side
                    far[k, row : row + 1, :] = jnp.sum(
                        summed[c * modes_y : (c + 1) * modes_y, cols] * ty, 0, keepdims=True
                    )
        value = far[k]
        return value * phi[k, 0] - times_i(value) * phi[k, 1]

    def near_field(halo):
        result = []
        for h in range(tiles):
            picked = []
            for j in range(9):
                slot = neighbor[0, h, j]
                row = slot // 3
                column = lax.rem(h + lax.rem(slot, 3) + tiles + 1, tiles + 2)
                picked.append(halo[row, column])
            left = jnp.concatenate(picked, 1)
            right = jnp.concatenate(
                [
                    jnp.concatenate([kernel_vmem[h, j, c] for j in range(9)], 0)
                    for c in range(2)
                ],
                1,
            )
            product = jnp.dot(left, right, preferred_element_type=f32)
            result.append(
                (
                    product[:vectors, :lanes] - product[vectors:, lanes:],
                    product[:vectors, lanes:] + product[vectors:, :lanes],
                )
            )
        return result

    pl.semaphore_wait(barrier, greeted)
    copies_1 = halo_copies(0, halo_1, edge_1)
    for copy in copies_1:
        start(copy)
    for k in reversed(range(vectors)):
        start(column_copy(phase_a, k, send_a.at[turn(k)], recv_a))

    for load in loads[2:6]:
        load.wait()
    my_weight = weight_vmem[frequency[mine]] * (1.0 / math.sqrt(modes_x * modes_y * panels))
    diagonal = jnp.sum(jnp.sum(my_weight, 0, keepdims=True), 1, keepdims=True)
    exact = lax.Precision.HIGHEST

    def pick(lattice, half):
        index = lax.broadcasted_iota(jnp.int32, (half, 2 * half), 0)
        given = jnp.broadcast_to(lattice[...], index.shape)
        plus = jnp.where(given == index + half, 1.0, 0.0)
        minus = jnp.where(given == half - 1 - index, 1.0, 0.0)
        return plus + minus, plus - minus

    even_y, odd_y = pick(lattice_y, half_y)
    even_x, odd_x = pick(lattice_x, half_x)
    by_y = rows_dot(jnp.concatenate([even_y, odd_y], 0), my_weight, exact)
    pick_x = jnp.concatenate([even_x, even_x, -odd_x, odd_x], 0)
    fact[...] = rows_dot(by_y, pick_x, exact)

    ahead = vectors // 2
    total = None

    def take(k):
        nonlocal total
        column_wait(phase_a, k, recv_a)
        given = tables(k)
        dense[k] = recv_a[turn(k), 0:rows, :].astype(bf16).astype(f32)
        total = add(total, project(k, dense[k], given))

    for k in range(ahead):
        take(k)

    def send_tiles(pairs, slab):
        for h in range(tiles):
            for c in range(2):
                slab[:, c * tiles + h, :] = pairs[h][c]

    for load in loads[6:]:
        load.wait()
    for copy in copies_1:
        copy.wait_recv()
    send_tiles(near_field(halo_1), send_n)
    for k in reversed(range(vectors)):
        start(column_copy(phase_n, k, send_n.at[turn(k)], recv_n))

    for k in range(ahead, vectors):
        take(k)

    def gather_sum(phase, source, target):
        if members == 2:
            return source[...] + target[lax.rem(member + 1, members)]
        target[member] = source[...]
        return jnp.sum(target[...], 0)

    send_g1[...] = both_sums(total)
    for k in range(1, members):
        start(mate_copy(0, k, send_g1, recv_g1))
    for k in range(1, members):
        mate_wait(0, k, recv_g1)
    weigh(gather_sum(0, send_g1, recv_g1))

    fields = [expand(k) for k in range(vectors)]
    def halo_message(k):
        u = turn(k)
        before = zeta[lax.rem(u + vectors - 1, vectors)]
        own = zeta[u]
        after = zeta[lax.rem(u + 1, vectors)]
        rounded = jnp.concatenate([before, own, after, after], 0).astype(bf16)
        send_h[k] = rounded
        start(column_copy(phase_h, k, send_h.at[k], recv_h))
        inner = (row_id == 1) | (row_id == tiles + 1)
        edge = inner | (row_id == tiles - 2) | (row_id == 2 * tiles - 2)
        moved = jnp.where(inner, pltpu.roll(own, 1, 0), pltpu.roll(own, 2 * tiles - 1, 0))
        rounded = jnp.concatenate([jnp.where(edge, moved, before), after], 0).astype(bf16)
        if k:
            send_o[k] = rounded
            start(column_copy(phase_o, k, send_o.at[k], recv_o, w))
        else:
            recv_o[mine] = rounded

    zero = jnp.zeros((rows, lanes), f32)
    sums = [zero] * 5
    total = None
    for k in range(vectors):
        column_wait(phase_n, k, recv_n)
        u = turn(k)
        given = recv_a[u, 0:rows, :]
        base = dense[k]
        value = fields[k] + recv_n[u] - diagonal * base
        zeta[u] = value
        turned = times_i(value)
        terms = (given * given, base * base, base * value, -base * turned, value * value)
        sums = [x + y for x, y in zip(sums, terms)]
        if sub > 1:
            send_z[k] = value
            start(column_copy(phase_z, k, send_z.at[k], recv_z))
        if sub == 1 and k == vectors - 1:
            for other in reversed(range(2, vectors)):
                halo_message(other)
        total = add(total, project(k, value))
    send_g2[0 : 2 * modes_y] = both_sums(total)
    line = jnp.zeros((rows, lanes), f32)
    for number, x in enumerate(sums):
        whole = jnp.sum(jnp.sum(x, 0, keepdims=True), 1, keepdims=True)
        line = jnp.where(row_id == number, whole, line)
    send_g2[2 * modes_y :] = line
    for k in range(1, members):
        start(mate_copy(1, k, send_g2, recv_g2))
    if sub == 1:
        for k in (1, 0):
            halo_message(k)

    if sub > 1:
        for k in range(vectors):
            column_wait(phase_z, k, recv_z)
        for h in range(tiles):
            pair = [recv_z[:, c * tiles + h, :].astype(bf16) for c in range(2)]
            put_halo(h, jnp.concatenate(pair, 0), halo_2, edge_2)
        copies_2 = halo_copies(1, halo_2, edge_2)
        for copy in copies_2:
            start(copy)

    for k in range(1, members):
        mate_wait(1, k, recv_g2)
    total = gather_sum(1, send_g2, recv_g2)
    weigh(total[0 : 2 * modes_y])
    line = total[2 * modes_y :]
    squares, base_sq, inner_r, inner_i, value_sq = [line[i : i + 1] for i in range(5)]
    shift = 0.5 + diagonal
    variance = squares / panels + eps_norm
    scale = jnp.sqrt(variance)
    over = 1.0 / (panels * variance)
    rest_r = (shift * base_sq + inner_r) * over
    coef_i = inner_i * over
    coef_r = rest_r
    move_r = coef_r - shift
    update_sq = (
        value_sq
        - 2.0 * (move_r * inner_r + coef_i * inner_i)
        + (move_r * move_r + coef_i * coef_i) * base_sq
    )
    update_scale = jnp.sqrt(jnp.maximum(update_sq, 0.0) * over + eps_norm)
    inverse = 1.0 / (scale * update_scale)
    lane_id = lax.broadcasted_iota(jnp.int32, (1, lanes), 1)
    result = jnp.zeros((1, lanes), f32)
    for number, x in enumerate((scale, coef_r, coef_i, update_scale, inverse)):
        result = jnp.where(lane_id == number, x, result)

    order = list(reversed(range(vectors)))
    field = expand(order[0])
    for number, k in enumerate(order):
        u = turn(k)
        if number and number + 1 < vectors:
            coming = expand(order[number + 1])
        value = zeta[u]
        image = value + shift * dense[k]
        out = field + 0.5 * value - move_r * image - coef_i * times_i(image)
        send_f[u, 0:rows, :] = out * inverse
        send_f[u, rows : rows + 1, :] = result
        start(column_copy(phase_f, k, send_f.at[u], recv_f))
        field = coming if number else expand(order[1])

    last = started[-vectors:]
    for copy in started[:-vectors]:
        copy.wait_send()
    if sub > 1:
        for copy in copies_2:
            copy.wait_recv()
    else:
        for k in range(vectors):
            column_wait(phase_h, k, recv_h)
            if k:
                column_wait(phase_o, k, recv_o)
        near_h[...] = recv_h[...].astype(f32)
        near_o[...] = recv_o[...].astype(f32)
        for strip in range(3):
            for h in range(tiles):
                first = strip * rows + h
                pair = [near_h[:, first + c * tiles, :] for c in range(2)]
                halo_2[strip, h] = jnp.concatenate(pair, 0).astype(bf16)
            for h in (0, tiles - 1):
                first = (h, 1 if h == 0 else h - 1, rows + h)[strip]
                pair = [near_o[:, first + c * tiles, :] for c in range(2)]
                halo_2[strip, tiles + h // (tiles - 1)] = jnp.concatenate(pair, 0).astype(bf16)
    near = near_field(halo_2)
    for k in range(vectors):
        column_wait(phase_f, k, recv_f)
    row = lax.broadcasted_iota(jnp.int32, (vectors, lanes), 0)
    lane = lax.broadcasted_iota(jnp.int32, (vectors, lanes), 1)
    scalars = recv_f[:, rows, :]
    columns = [
        jnp.sum(jnp.where(lane == number, scalars, 0.0), 1, keepdims=True) for number in range(5)
    ]
    scaling = columns[4]
    for h in range(tiles):
        for c in range(2):
            image_out[h, c] = recv_f[:, c * tiles + h, :] + near[h][c] * scaling
    for number in range(4):
        line = jnp.sum(jnp.where(row == lane, columns[number], 0.0), 0, keepdims=True)
        arnoldi_out[number : number + 1, :] = line[:, :vectors]

    for copy in last:
        copy.wait_send()


def hand_over(image, arnoldi, image_out, arnoldi_out):
    image_out[...] = image[...]
    arnoldi_out[...] = arnoldi[...]


def per_device(
    size_t,
    size_w,
    residual,
    kernel,
    offsets,
    neighbor,
    frequency,
    lattice_x,
    lattice_y,
    spectral_weight,
):
    strips, tiles, _, vectors, lanes = residual.shape
    modes_x, modes_y = spectral_weight.shape[1:]
    assert strips == 1 and lanes == 128 and size_w == 2 and size_t > 2
    assert size_t % vectors == 0 and tiles == 4 and vectors == 8
    assert modes_x == 128 and modes_y == 128
    members = size_w * (size_t // vectors)
    rows = 2 * tiles
    vmem = pl.BlockSpec(memory_space=pltpu.VMEM)
    anywhere = pl.BlockSpec(memory_space=pl.ANY)
    halo = pltpu.VMEM((3, tiles + 2, 2 * vectors, lanes), bf16)
    edge = pltpu.VMEM((2, 2 * vectors, lanes), bf16)
    wide = pltpu.VMEM((vectors, 2 * rows, lanes), f32)
    slim = pltpu.VMEM((vectors, rows, lanes), f32)
    image, arnoldi = pl.pallas_call(
        functools.partial(body, size_t, size_w, tiles, vectors, modes_x, modes_y),
        out_shape=(
            pltpu.VMEM((tiles, 2, vectors, lanes), f32),
            pltpu.VMEM((4, vectors), f32),
        ),
        in_specs=[anywhere] * 8,
        out_specs=(vmem, vmem),
        scratch_shapes=[
            wide,
            wide,
            slim,
            slim,
            slim,
            slim,
            pltpu.VMEM((vectors, 4 * rows, lanes), bf16),
            pltpu.VMEM((vectors, 4 * rows, lanes), bf16),
            pltpu.VMEM((vectors, 2 * rows, lanes), bf16),
            pltpu.VMEM((vectors, 2 * rows, lanes), bf16),
            pltpu.VMEM((vectors, 4 * rows, lanes), f32),
            wide,
            pltpu.VMEM((vectors, rows + 1, lanes), f32),
            pltpu.VMEM((vectors, rows + 1, lanes), f32),
            pltpu.VMEM((2 * modes_y, modes_x), f32),
            pltpu.VMEM((members, 2 * modes_y, modes_x), f32),
            pltpu.VMEM((2 * modes_y + rows, modes_x), f32),
            pltpu.VMEM((members, 2 * modes_y + rows, modes_x), f32),
            halo,
            halo,
            edge,
            edge,
            pltpu.VMEM((vectors, tiles, modes_x, lanes), bf16),
            pltpu.VMEM((vectors, tiles, modes_y, lanes), bf16),
            pltpu.VMEM((vectors, tiles, modes_y, lanes), f32),
            pltpu.VMEM((vectors, 2, rows, lanes), f32),
            slim,
            slim,
            slim,
            pltpu.VMEM((modes_y, 2 * modes_x), f32),
            pltpu.VMEM((2, 2 * modes_y, modes_x), bf16),
            pltpu.VMEM((2, 2 * modes_y, modes_x), f32),
            pltpu.VMEM(residual.shape[1:], f32),
            pltpu.VMEM(offsets.shape[1:], f32),
            pltpu.SMEM(neighbor.shape, jnp.int32),
            pltpu.SMEM(frequency.shape, jnp.int32),
            pltpu.VMEM((1, modes_x), jnp.int32),
            pltpu.VMEM((1, modes_y), jnp.int32),
            pltpu.VMEM((tiles, 9, 2, lanes, lanes), bf16),
            pltpu.VMEM(spectral_weight.shape, f32),
            pltpu.SemaphoreType.DMA((8,)),
            pltpu.SemaphoreType.DMA((6, vectors)),
            pltpu.SemaphoreType.DMA((6, vectors)),
            pltpu.SemaphoreType.DMA((2, members)),
            pltpu.SemaphoreType.DMA((2, members)),
            pltpu.SemaphoreType.DMA((2, 5)),
            pltpu.SemaphoreType.DMA((2, 5)),
        ],
        compiler_params=pltpu.CompilerParams(
            collective_id=0, has_side_effects=True, vmem_limit_bytes=56 * 1024 * 1024
        ),
        name="arnoldi_pair",
    )(
        residual[0],
        kernel[0],
        offsets[0],
        neighbor,
        frequency,
        lattice_x[None],
        lattice_y[None],
        spectral_weight,
    )
    image, arnoldi = [
        pltpu.with_memory_space_constraint(x, pltpu.VMEM) for x in (image, arnoldi)
    ]
    image, arnoldi = pl.pallas_call(
        hand_over,
        out_shape=(
            jax.ShapeDtypeStruct(image.shape, f32),
            jax.ShapeDtypeStruct(arnoldi.shape, f32),
        ),
        in_specs=[vmem, vmem],
        out_specs=(vmem, vmem),
        name="hand_over",
    )(image, arnoldi)
    return image[None], arnoldi


def solution(mesh):
    return jax.shard_map(
        functools.partial(per_device, mesh.shape["tile"], mesh.shape["wave"]),
        mesh=mesh,
        in_specs=(
            P(("grp", "tile"), "wave", None, None, None),
            P(("grp", "tile"), "wave", None, None, None, None),
            P(("grp", "tile"), "wave", None, None),
            P(("grp", "tile"), "wave", None),
            P("grp"),
            P(),
            P(),
            P(),
        ),
        out_specs=(P(("grp", "tile"), "wave", None, None, None), P("grp", None)),
        check_vma=False,
    )
```

```python
import functools
import math

import jax
import jax.numpy as jnp
from jax import lax
from jax.experimental import pallas as pl
from jax.experimental.pallas import tpu as pltpu
from jax.sharding import PartitionSpec as P

eps_norm = 1e-06
f32 = jnp.float32
bf16 = jnp.bfloat16
MESH = pl.DeviceIdType.MESH
phase_a, phase_n, phase_z, phase_f, phase_h, phase_o = range(6)

cos_poly = (
    0.9999992107823232,
    -19.73898035576408,
    64.9286574210355,
    -85.2716215343227,
    58.79049212023139,
    -21.071105627794083,
)
sin_poly = (
    6.283184916495429,
    -41.34158923268887,
    81.59994332979169,
    -76.61447253134614,
    41.34288235500671,
    -12.471243535733244,
)


def horner(coefs, z):
    total = coefs[-1] * z + coefs[-2]
    for c in coefs[-3::-1]:
        total = total * z + c
    return total


def cos_sin(turns):
    r = turns - jnp.round(turns)
    z = r * r
    return horner(cos_poly, z), r * horner(sin_poly, z)


def rows_dot(a, b, precision=None):
    return lax.dot_general(
        a, b, (((1,), (1,)), ((), ())), precision=precision, preferred_element_type=f32
    )


def body(
    size_t,
    size_w,
    tiles,
    vectors,
    modes_x,
    modes_y,
    residual_any,
    blocks,
    offsets_any,
    neighbor_any,
    frequency_any,
    lattice_x_any,
    lattice_y_any,
    weight,
    image_out,
    arnoldi_out,
    send_a,
    recv_a,
    send_n,
    recv_n,
    send_z,
    recv_z,
    send_h,
    recv_h,
    send_o,
    recv_o,
    near_h,
    near_o,
    send_f,
    recv_f,
    send_g1,
    recv_g1,
    send_g2,
    recv_g2,
    halo_1,
    halo_2,
    edge_1,
    edge_2,
    table_x,
    table_y,
    wide_y,
    phi,
    dense,
    zeta,
    far,
    fact,
    coeffs,
    halves,
    residual,
    offsets,
    neighbor,
    frequency,
    lattice_x,
    lattice_y,
    kernel_vmem,
    weight_vmem,
    load_sem,
    col_send,
    col_recv,
    mate_send,
    mate_recv,
    halo_send,
    halo_recv,
):
    devices = size_t * size_w
    sub = size_t // vectors
    members = size_w * sub
    rows = 2 * tiles
    half_x = modes_x // 2
    half_y = modes_y // 2
    lanes = 128
    panels = devices * tiles * lanes
    count_x = size_t
    count_y = size_w * tiles
    t = lax.axis_index("tile")
    w = lax.axis_index("wave")
    me = t * size_w + w
    mine = t // sub
    part = lax.rem(t, sub)
    member = part * size_w + w

    up = lax.rem(t + 1, size_t)
    down = lax.rem(t + size_t - 1, size_t)
    other_w = lax.rem(w + 1, size_w)

    barrier = pltpu.get_barrier_semaphore()

    def greet(to_t, to_w):
        place = {"tile": to_t, "wave": to_w}
        pl.semaphore_signal(barrier, inc=1, device_id=place, device_id_type=MESH)

    if sub == 1:
        greeted = vectors + 2
        greet(up, w)
        greet(down, w)
        for k in range(vectors):
            greet(lax.rem(t + k, size_t), other_w)
    else:
        greeted = devices - 1

        def greet_one(k, carry):
            other = lax.rem(me + k, devices)
            greet(other // size_w, lax.rem(other, size_w))
            return carry

        lax.fori_loop(1, devices, greet_one, 0)

    loads = []
    for number, (source, target) in enumerate(
        (
            (residual_any, residual),
            (offsets_any, offsets),
            (frequency_any, frequency),
            (weight, weight_vmem),
            (lattice_x_any, lattice_x),
            (lattice_y_any, lattice_y),
            (neighbor_any, neighbor),
            (blocks, kernel_vmem),
        )
    ):
        loads.append(pltpu.make_async_copy(source, target, load_sem.at[number]))
        loads[-1].start()

    bits = [lax.rem(mine // (1 << i), 2) for i in range(3)]

    def turn(k):
        return sum(((1 - b) if (k >> i) & 1 else b) * (1 << i) for i, b in enumerate(bits))

    def column_copy(phase, k, source, target, wave=None):
        return pltpu.make_async_remote_copy(
            src_ref=source,
            dst_ref=target.at[mine],
            send_sem=col_send.at[phase, k],
            recv_sem=col_recv.at[phase, k],
            device_id={"tile": turn(k) * sub + part, "wave": other_w if wave is None else wave},
            device_id_type=MESH,
        )

    def column_wait(phase, k, target):
        slot = target.at[turn(k)]
        pltpu.make_async_copy(slot, slot, col_recv.at[phase, k]).wait()

    def mate_copy(phase, k, source, target):
        other = lax.rem(member + k, members)
        return pltpu.make_async_remote_copy(
            src_ref=source,
            dst_ref=target.at[member],
            send_sem=mate_send.at[phase, k],
            recv_sem=mate_recv.at[phase, members - k],
            device_id={"tile": mine * sub + other // size_w, "wave": lax.rem(other, size_w)},
            device_id_type=MESH,
        )

    def mate_wait(phase, k, target):
        slot = target.at[lax.rem(member + k, members)]
        pltpu.make_async_copy(slot, slot, mate_recv.at[phase, k]).wait()

    def halo_copies(phase, halo, edge):
        copies = []
        targets = ((down, w, 2), (down, other_w, 2), (up, w, 0), (up, other_w, 0), (t, other_w, 1))
        for number, (to_t, to_w, row) in enumerate(targets):
            own = number in (0, 2)
            copies.append(
                pltpu.make_async_remote_copy(
                    src_ref=halo.at[1, pl.ds(0, tiles)] if own else edge,
                    dst_ref=halo.at[row, pl.ds(0, tiles) if own else pl.ds(tiles, 2)],
                    send_sem=halo_send.at[phase, number],
                    recv_sem=halo_recv.at[phase, number],
                    device_id={"tile": to_t, "wave": to_w},
                    device_id_type=MESH,
                )
            )
        return copies

    def put_halo(h, value, halo, edge):
        halo[1, h] = value
        if h in (0, tiles - 1):
            edge[h // (tiles - 1)] = value

    started = []

    def start(copy):
        copy.start()
        started.append(copy)

    row_id = lax.broadcasted_iota(jnp.int32, (rows, lanes), 0)
    upper = row_id < tiles
    sign = jnp.where(upper, -1.0, 1.0)

    def times_i(x):
        return pltpu.roll(x, tiles, 0) * sign

    loads[0].wait()
    loads[1].wait()
    offset_rows = jnp.concatenate([offsets[:, 0, :], offsets[:, 1, :]], 0)
    for h in range(tiles):
        rounded = []
        for c in range(2):
            value = residual[h, c]
            send_a[:, c * tiles + h, :] = value
            rounded.append(value.astype(bf16))
        put_halo(h, jnp.concatenate(rounded, 0), halo_1, edge_1)
    for v in range(vectors):
        send_a[v, rows : 2 * rows, :] = offset_rows

    low = lax.broadcasted_iota(jnp.int32, (8, lanes), 0).astype(f32) + 0.5
    count = jnp.where(upper, float(count_x), float(count_y))
    tile_row = (row_id - tiles + other_w * tiles).astype(f32)

    def harmonics(position, cos_8, sin_8):
        cos_b, sin_b = cos_sin(position * low)
        cosines = [cos_b, cos_b * cos_8 - sin_b * sin_8]
        sines = [sin_b, sin_b * cos_8 + cos_b * sin_8]
        twice = cos_8 + cos_8
        for series in (cosines, sines):
            for m in range(2, 8):
                series.append(twice * series[-1] - series[-2])
        return jnp.concatenate(cosines + sines, 0)

    def tables(k):
        u = turn(k)
        off = recv_a[u, rows : 2 * rows, :]
        strip = (u * sub + part).astype(f32)
        pos = (jnp.where(upper, strip, tile_row) + off) / count
        cos_p, sin_p = cos_sin(0.5 * (pos + pltpu.roll(pos, tiles, 0)))
        cos_8, sin_8 = cos_sin(8.0 * pos)
        phi[k, 0] = cos_p
        phi[k, 1] = sin_p
        given = []
        for h in range(tiles):
            tx = harmonics(*[jnp.broadcast_to(x[h : h + 1], (8, lanes)) for x in (pos, cos_8, sin_8)])
            table_x[k, h] = tx.astype(bf16)
            row = tiles + h
            ty = harmonics(
                *[jnp.broadcast_to(x[row : row + 1], (8, lanes)) for x in (pos, cos_8, sin_8)]
            )
            table_y[k, h] = ty.astype(bf16)
            wide_y[k, h] = ty
            given.append(ty.astype(bf16))
        return given

    def add(totals, terms):
        return terms if totals is None else [x + y for x, y in zip(totals, terms)]

    def project(k, density, given=None):
        rotated = density * phi[k, 0] + times_i(density) * phi[k, 1]
        twisted = []
        for h in range(tiles):
            ty = table_y[k, h] if given is None else given[h]
            both = []
            for c in range(2):
                row = c * tiles + h
                q = jnp.broadcast_to(rotated[row : row + 1], (16, lanes)).astype(bf16)
                both.append(ty * jnp.concatenate([q] * (modes_y // 16), 0))
            twisted.append(jnp.concatenate(both, 0))
        return [
            rows_dot(
                jnp.concatenate(twisted[h : h + 2], 1),
                jnp.concatenate([table_x[k, h], table_x[k, h + 1]], 1),
            )
            for h in range(0, tiles, 2)
        ]

    def both_sums(totals):
        halves[w] = totals[0]
        halves[other_w] = totals[1]
        return halves[0] + halves[1]

    def weigh(total):
        x_r, y_r = total[0:half_y], total[half_y:modes_y]
        x_i, y_i = total[modes_y : modes_y + half_y], total[modes_y + half_y :]
        rx_r, ry_r, rx_i, ry_i = [pltpu.roll(x, half_x, 1) for x in (x_r, y_r, x_i, y_i)]
        f_0 = fact[0:half_y, 0:modes_x]
        f_s = fact[0:half_y, modes_x:]
        f_t = fact[half_y:, 0:modes_x]
        f_1 = fact[half_y:, modes_x:]
        matrix = jnp.concatenate(
            [
                f_0 * x_r + f_1 * ry_r - f_s * rx_i + f_t * y_i,
                f_0 * y_r - f_1 * rx_r - f_t * x_i - f_s * ry_i,
                f_0 * x_i + f_1 * ry_i + f_s * rx_r - f_t * y_r,
                f_0 * y_i - f_1 * rx_i + f_t * x_r + f_s * ry_r,
            ],
            0,
        ).astype(bf16)
        coeffs[w] = matrix
        coeffs[other_w] = matrix

    def expand(k):
        for h in range(0, tiles, 2):
            summed = jnp.dot(
                coeffs[(w, other_w)[h // 2]],
                jnp.concatenate([table_x[k, h], table_x[k, h + 1]], 1),
                preferred_element_type=f32,
            )
            for side in range(2):
                cols = slice(side * lanes, (side + 1) * lanes)
                ty = wide_y[k, h + side]
                for c in range(2):
                    row = c * tiles + h + side
                    far[k, row : row + 1, :] = jnp.sum(
                        summed[c * modes_y : (c + 1) * modes_y, cols] * ty, 0, keepdims=True
                    )
        value = far[k]
        return value * phi[k, 0] - times_i(value) * phi[k, 1]

    def near_field(halo):
        result = []
        for h in range(tiles):
            picked = []
            for j in range(9):
                slot = neighbor[0, h, j]
                row = slot // 3
                column = lax.rem(h + lax.rem(slot, 3) + tiles + 1, tiles + 2)
                picked.append(halo[row, column])
            left = jnp.concatenate(picked, 1)
            right = jnp.concatenate(
                [
                    jnp.concatenate([kernel_vmem[h, j, c] for j in range(9)], 0)
                    for c in range(2)
                ],
                1,
            )
            product = jnp.dot(left, right, preferred_element_type=f32)
            result.append(
                (
                    product[:vectors, :lanes] - product[vectors:, lanes:],
                    product[:vectors, lanes:] + product[vectors:, :lanes],
                )
            )
        return result

    pl.semaphore_wait(barrier, greeted)
    copies_1 = halo_copies(0, halo_1, edge_1)
    for copy in copies_1:
        start(copy)
    for k in reversed(range(vectors)):
        start(column_copy(phase_a, k, send_a.at[turn(k)], recv_a))

    for load in loads[2:6]:
        load.wait()
    my_weight = weight_vmem[frequency[mine]] * (1.0 / math.sqrt(modes_x * modes_y * panels))
    diagonal = jnp.sum(jnp.sum(my_weight, 0, keepdims=True), 1, keepdims=True)
    exact = lax.Precision.HIGHEST

    def pick(lattice, half):
        index = lax.broadcasted_iota(jnp.int32, (half, 2 * half), 0)
        given = jnp.broadcast_to(lattice[...], index.shape)
        plus = jnp.where(given == index + half, 1.0, 0.0)
        minus = jnp.where(given == half - 1 - index, 1.0, 0.0)
        return plus + minus, plus - minus

    even_y, odd_y = pick(lattice_y, half_y)
    even_x, odd_x = pick(lattice_x, half_x)
    by_y = rows_dot(jnp.concatenate([even_y, odd_y], 0), my_weight, exact)
    pick_x = jnp.concatenate([even_x, even_x, -odd_x, odd_x], 0)
    fact[...] = rows_dot(by_y, pick_x, exact)

    ahead = vectors // 2
    total = None

    def take(k):
        nonlocal total
        column_wait(phase_a, k, recv_a)
        given = tables(k)
        dense[k] = recv_a[turn(k), 0:rows, :].astype(bf16).astype(f32)
        total = add(total, project(k, dense[k], given))

    for k in range(ahead):
        take(k)

    def send_tiles(pairs, slab):
        for h in range(tiles):
            for c in range(2):
                slab[:, c * tiles + h, :] = pairs[h][c]

    for load in loads[6:]:
        load.wait()
    for copy in copies_1:
        copy.wait_recv()
    send_tiles(near_field(halo_1), send_n)
    for k in reversed(range(vectors)):
        start(column_copy(phase_n, k, send_n.at[turn(k)], recv_n))

    for k in range(ahead, vectors):
        take(k)

    def gather_sum(phase, source, target):
        if members == 2:
            return source[...] + target[lax.rem(member + 1, members)]
        target[member] = source[...]
        return jnp.sum(target[...], 0)

    send_g1[...] = both_sums(total)
    for k in range(1, members):
        start(mate_copy(0, k, send_g1, recv_g1))
    for k in range(1, members):
        mate_wait(0, k, recv_g1)
    weigh(gather_sum(0, send_g1, recv_g1))

    fields = [expand(k) for k in range(vectors)]
    def halo_message(k):
        u = turn(k)
        before = zeta[lax.rem(u + vectors - 1, vectors)]
        own = zeta[u]
        after = zeta[lax.rem(u + 1, vectors)]
        rounded = jnp.concatenate([before, own, after, after], 0).astype(bf16)
        send_h[k] = rounded
        start(column_copy(phase_h, k, send_h.at[k], recv_h))
        inner = (row_id == 1) | (row_id == tiles + 1)
        edge = inner | (row_id == tiles - 2) | (row_id == 2 * tiles - 2)
        moved = jnp.where(inner, pltpu.roll(own, 1, 0), pltpu.roll(own, 2 * tiles - 1, 0))
        rounded = jnp.concatenate([jnp.where(edge, moved, before), after], 0).astype(bf16)
        if k:
            send_o[k] = rounded
            start(column_copy(phase_o, k, send_o.at[k], recv_o, w))
        else:
            recv_o[mine] = rounded

    zero = jnp.zeros((rows, lanes), f32)
    sums = [zero] * 5
    total = None
    for k in range(vectors):
        column_wait(phase_n, k, recv_n)
        u = turn(k)
        given = recv_a[u, 0:rows, :]
        base = dense[k]
        value = fields[k] + recv_n[u] - diagonal * base
        zeta[u] = value
        turned = times_i(value)
        terms = (given * given, base * base, base * value, -base * turned, value * value)
        sums = [x + y for x, y in zip(sums, terms)]
        if sub > 1:
            send_z[k] = value
            start(column_copy(phase_z, k, send_z.at[k], recv_z))
        if sub == 1 and k == vectors - 1:
            for other in reversed(range(2, vectors)):
                halo_message(other)
        total = add(total, project(k, value))
    send_g2[0 : 2 * modes_y] = both_sums(total)
    line = jnp.zeros((rows, lanes), f32)
    for number, x in enumerate(sums):
        whole = jnp.sum(jnp.sum(x, 0, keepdims=True), 1, keepdims=True)
        line = jnp.where(row_id == number, whole, line)
    send_g2[2 * modes_y :] = line
    for k in range(1, members):
        start(mate_copy(1, k, send_g2, recv_g2))
    if sub == 1:
        for k in (1, 0):
            halo_message(k)

    if sub > 1:
        for k in range(vectors):
            column_wait(phase_z, k, recv_z)
        for h in range(tiles):
            pair = [recv_z[:, c * tiles + h, :].astype(bf16) for c in range(2)]
            put_halo(h, jnp.concatenate(pair, 0), halo_2, edge_2)
        copies_2 = halo_copies(1, halo_2, edge_2)
        for copy in copies_2:
            start(copy)

    for k in range(1, members):
        mate_wait(1, k, recv_g2)
    total = gather_sum(1, send_g2, recv_g2)
    weigh(total[0 : 2 * modes_y])
    line = total[2 * modes_y :]
    squares, base_sq, inner_r, inner_i, value_sq = [line[i : i + 1] for i in range(5)]
    shift = 0.5 + diagonal
    variance = squares / panels + eps_norm
    scale = jnp.sqrt(variance)
    over = 1.0 / (panels * variance)
    rest_r = (shift * base_sq + inner_r) * over
    coef_i = inner_i * over
    coef_r = rest_r
    move_r = coef_r - shift
    update_sq = (
        value_sq
        - 2.0 * (move_r * inner_r + coef_i * inner_i)
        + (move_r * move_r + coef_i * coef_i) * base_sq
    )
    update_scale = jnp.sqrt(jnp.maximum(update_sq, 0.0) * over + eps_norm)
    inverse = 1.0 / (scale * update_scale)
    lane_id = lax.broadcasted_iota(jnp.int32, (1, lanes), 1)
    result = jnp.zeros((1, lanes), f32)
    for number, x in enumerate((scale, coef_r, coef_i, update_scale, inverse)):
        result = jnp.where(lane_id == number, x, result)
    result = jnp.broadcast_to(result, (rows, lanes))

    order = list(reversed(range(vectors)))
    field = expand(order[0])
    for number, k in enumerate(order):
        u = turn(k)
        if number and number + 1 < vectors:
            coming = expand(order[number + 1])
        value = zeta[u]
        image = value + shift * dense[k]
        out = field + 0.5 * value - move_r * image - coef_i * times_i(image)
        send_f[u, 0:rows, :] = out * inverse
        send_f[u, rows : 2 * rows, :] = result
        start(column_copy(phase_f, k, send_f.at[u], recv_f))
        field = coming if number else expand(order[1])

    last = started[-vectors:]
    for copy in started[:-vectors]:
        copy.wait_send()
    if sub > 1:
        for copy in copies_2:
            copy.wait_recv()
    else:
        for k in range(vectors):
            column_wait(phase_h, k, recv_h)
            if k:
                column_wait(phase_o, k, recv_o)
        near_h[...] = recv_h[...].astype(f32)
        near_o[...] = recv_o[...].astype(f32)
        for strip in range(3):
            for h in range(tiles):
                first = strip * rows + h
                pair = [near_h[:, first + c * tiles, :] for c in range(2)]
                halo_2[strip, h] = jnp.concatenate(pair, 0).astype(bf16)
            for h in (0, tiles - 1):
                first = (h, 1 if h == 0 else h - 1, rows + h)[strip]
                pair = [near_o[:, first + c * tiles, :] for c in range(2)]
                halo_2[strip, tiles + h // (tiles - 1)] = jnp.concatenate(pair, 0).astype(bf16)
    near = near_field(halo_2)
    for k in range(vectors):
        column_wait(phase_f, k, recv_f)
    row = lax.broadcasted_iota(jnp.int32, (vectors, lanes), 0)
    lane = lax.broadcasted_iota(jnp.int32, (vectors, lanes), 1)
    scalars = recv_f[:, rows, :]
    columns = [
        jnp.sum(jnp.where(lane == number, scalars, 0.0), 1, keepdims=True) for number in range(5)
    ]
    scaling = columns[4]
    for h in range(tiles):
        for c in range(2):
            image_out[h, c] = recv_f[:, c * tiles + h, :] + near[h][c] * scaling
    for number in range(4):
        line = jnp.sum(jnp.where(row == lane, columns[number], 0.0), 0, keepdims=True)
        arnoldi_out[number : number + 1, :] = line[:, :vectors]

    for copy in last:
        copy.wait_send()


def hand_over(image, arnoldi, image_out, arnoldi_out):
    image_out[...] = image[...]
    arnoldi_out[...] = arnoldi[...]


def per_device(
    size_t,
    size_w,
    residual,
    kernel,
    offsets,
    neighbor,
    frequency,
    lattice_x,
    lattice_y,
    spectral_weight,
):
    strips, tiles, _, vectors, lanes = residual.shape
    modes_x, modes_y = spectral_weight.shape[1:]
    assert strips == 1 and lanes == 128 and size_w == 2 and size_t > 2
    assert size_t % vectors == 0 and tiles == 4 and vectors == 8
    assert modes_x == 128 and modes_y == 128
    members = size_w * (size_t // vectors)
    rows = 2 * tiles
    vmem = pl.BlockSpec(memory_space=pltpu.VMEM)
    anywhere = pl.BlockSpec(memory_space=pl.ANY)
    halo = pltpu.VMEM((3, tiles + 2, 2 * vectors, lanes), bf16)
    edge = pltpu.VMEM((2, 2 * vectors, lanes), bf16)
    wide = pltpu.VMEM((vectors, 2 * rows, lanes), f32)
    slim = pltpu.VMEM((vectors, rows, lanes), f32)
    image, arnoldi = pl.pallas_call(
        functools.partial(body, size_t, size_w, tiles, vectors, modes_x, modes_y),
        out_shape=(
            pltpu.VMEM((tiles, 2, vectors, lanes), f32),
            pltpu.VMEM((4, vectors), f32),
        ),
        in_specs=[anywhere] * 8,
        out_specs=(vmem, vmem),
        scratch_shapes=[
            wide,
            wide,
            slim,
            slim,
            slim,
            slim,
            pltpu.VMEM((vectors, 4 * rows, lanes), bf16),
            pltpu.VMEM((vectors, 4 * rows, lanes), bf16),
            pltpu.VMEM((vectors, 2 * rows, lanes), bf16),
            pltpu.VMEM((vectors, 2 * rows, lanes), bf16),
            pltpu.VMEM((vectors, 4 * rows, lanes), f32),
            wide,
            wide,
            wide,
            pltpu.VMEM((2 * modes_y, modes_x), f32),
            pltpu.VMEM((members, 2 * modes_y, modes_x), f32),
            pltpu.VMEM((2 * modes_y + rows, modes_x), f32),
            pltpu.VMEM((members, 2 * modes_y + rows, modes_x), f32),
            halo,
            halo,
            edge,
            edge,
            pltpu.VMEM((vectors, tiles, modes_x, lanes), bf16),
            pltpu.VMEM((vectors, tiles, modes_y, lanes), bf16),
            pltpu.VMEM((vectors, tiles, modes_y, lanes), f32),
            pltpu.VMEM((vectors, 2, rows, lanes), f32),
            slim,
            slim,
            slim,
            pltpu.VMEM((modes_y, 2 * modes_x), f32),
            pltpu.VMEM((2, 2 * modes_y, modes_x), bf16),
            pltpu.VMEM((2, 2 * modes_y, modes_x), f32),
            pltpu.VMEM(residual.shape[1:], f32),
            pltpu.VMEM(offsets.shape[1:], f32),
            pltpu.SMEM(neighbor.shape, jnp.int32),
            pltpu.SMEM(frequency.shape, jnp.int32),
            pltpu.VMEM((1, modes_x), jnp.int32),
            pltpu.VMEM((1, modes_y), jnp.int32),
            pltpu.VMEM((tiles, 9, 2, lanes, lanes), bf16),
            pltpu.VMEM(spectral_weight.shape, f32),
            pltpu.SemaphoreType.DMA((8,)),
            pltpu.SemaphoreType.DMA((6, vectors)),
            pltpu.SemaphoreType.DMA((6, vectors)),
            pltpu.SemaphoreType.DMA((2, members)),
            pltpu.SemaphoreType.DMA((2, members)),
            pltpu.SemaphoreType.DMA((2, 5)),
            pltpu.SemaphoreType.DMA((2, 5)),
        ],
        compiler_params=pltpu.CompilerParams(
            collective_id=0, has_side_effects=True, vmem_limit_bytes=56 * 1024 * 1024
        ),
        name="arnoldi_pair",
    )(
        residual[0],
        kernel[0],
        offsets[0],
        neighbor,
        frequency,
        lattice_x[None],
        lattice_y[None],
        spectral_weight,
    )
    image, arnoldi = [
        pltpu.with_memory_space_constraint(x, pltpu.VMEM) for x in (image, arnoldi)
    ]
    image, arnoldi = pl.pallas_call(
        hand_over,
        out_shape=(
            jax.ShapeDtypeStruct(image.shape, f32),
            jax.ShapeDtypeStruct(arnoldi.shape, f32),
        ),
        in_specs=[vmem, vmem],
        out_specs=(vmem, vmem),
        name="hand_over",
    )(image, arnoldi)
    return image[None], arnoldi


def solution(mesh):
    return jax.shard_map(
        functools.partial(per_device, mesh.shape["tile"], mesh.shape["wave"]),
        mesh=mesh,
        in_specs=(
            P(("grp", "tile"), "wave", None, None, None),
            P(("grp", "tile"), "wave", None, None, None, None),
            P(("grp", "tile"), "wave", None, None),
            P(("grp", "tile"), "wave", None),
            P("grp"),
            P(),
            P(),
            P(),
        ),
        out_specs=(P(("grp", "tile"), "wave", None, None, None), P("grp", None)),
        check_vma=False,
    )
```

```python
import functools
import math

import jax
import jax.numpy as jnp
from jax import lax
from jax.experimental import pallas as pl
from jax.experimental.pallas import tpu as pltpu
from jax.sharding import PartitionSpec as P

eps_norm = 1e-06
f32 = jnp.float32
bf16 = jnp.bfloat16
MESH = pl.DeviceIdType.MESH
phase_a, phase_n, phase_z, phase_f, phase_h, phase_o = range(6)

cos_poly = (
    0.9999992107823232,
    -19.73898035576408,
    64.9286574210355,
    -85.2716215343227,
    58.79049212023139,
    -21.071105627794083,
)
sin_poly = (
    6.283184916495429,
    -41.34158923268887,
    81.59994332979169,
    -76.61447253134614,
    41.34288235500671,
    -12.471243535733244,
)


def horner(coefs, z):
    total = coefs[-1] * z + coefs[-2]
    for c in coefs[-3::-1]:
        total = total * z + c
    return total


def cos_sin(turns):
    r = turns - jnp.round(turns)
    z = r * r
    return horner(cos_poly, z), r * horner(sin_poly, z)


def rows_dot(a, b, precision=None):
    return lax.dot_general(
        a, b, (((1,), (1,)), ((), ())), precision=precision, preferred_element_type=f32
    )


def body(
    size_t,
    size_w,
    tiles,
    vectors,
    modes_x,
    modes_y,
    residual_any,
    blocks,
    offsets_any,
    neighbor_any,
    frequency_any,
    lattice_x_any,
    lattice_y_any,
    weight,
    image_out,
    arnoldi_out,
    send_a,
    recv_a,
    send_n,
    recv_n,
    send_z,
    recv_z,
    send_h,
    recv_h,
    send_o,
    recv_o,
    near_h,
    near_o,
    send_f,
    recv_f,
    send_g1,
    recv_g1,
    send_g2,
    recv_g2,
    halo_1,
    halo_2,
    edge_1,
    edge_2,
    table_x,
    table_y,
    wide_y,
    phi,
    dense,
    zeta,
    far,
    fact,
    coeffs,
    halves,
    residual,
    offsets,
    neighbor,
    frequency,
    lattice_x,
    lattice_y,
    kernel_vmem,
    weight_vmem,
    load_sem,
    col_send,
    col_recv,
    mate_send,
    mate_recv,
    halo_send,
    halo_recv,
):
    devices = size_t * size_w
    sub = size_t // vectors
    members = size_w * sub
    rows = 2 * tiles
    half_x = modes_x // 2
    half_y = modes_y // 2
    lanes = 128
    panels = devices * tiles * lanes
    count_x = size_t
    count_y = size_w * tiles
    t = lax.axis_index("tile")
    w = lax.axis_index("wave")
    me = t * size_w + w
    mine = t // sub
    part = lax.rem(t, sub)
    member = part * size_w + w

    up = lax.rem(t + 1, size_t)
    down = lax.rem(t + size_t - 1, size_t)
    other_w = lax.rem(w + 1, size_w)

    barrier = pltpu.get_barrier_semaphore()

    def greet(to_t, to_w):
        place = {"tile": to_t, "wave": to_w}
        pl.semaphore_signal(barrier, inc=1, device_id=place, device_id_type=MESH)

    if sub == 1:
        greeted = vectors + 2
        greet(up, w)
        greet(down, w)
        for k in range(vectors):
            greet(lax.rem(t + k, size_t), other_w)
    else:
        greeted = devices - 1

        def greet_one(k, carry):
            other = lax.rem(me + k, devices)
            greet(other // size_w, lax.rem(other, size_w))
            return carry

        lax.fori_loop(1, devices, greet_one, 0)

    loads = []
    for number, (source, target) in enumerate(
        (
            (residual_any, residual),
            (offsets_any, offsets),
            (frequency_any, frequency),
            (weight, weight_vmem),
            (lattice_x_any, lattice_x),
            (lattice_y_any, lattice_y),
            (neighbor_any, neighbor),
            (blocks, kernel_vmem),
        )
    ):
        loads.append(pltpu.make_async_copy(source, target, load_sem.at[number]))
        loads[-1].start()

    bits = [lax.rem(mine // (1 << i), 2) for i in range(3)]

    def turn(k):
        return sum(((1 - b) if (k >> i) & 1 else b) * (1 << i) for i, b in enumerate(bits))

    def part_of(phase, buffer, index):
        return buffer.at[index, pl.ds(0, rows + 1)] if phase == phase_f else buffer.at[index]

    def column_copy(phase, k, source, target, wave=None):
        return pltpu.make_async_remote_copy(
            src_ref=source,
            dst_ref=part_of(phase, target, mine),
            send_sem=col_send.at[phase, k],
            recv_sem=col_recv.at[phase, k],
            device_id={"tile": turn(k) * sub + part, "wave": other_w if wave is None else wave},
            device_id_type=MESH,
        )

    def column_wait(phase, k, target):
        slot = part_of(phase, target, turn(k))
        pltpu.make_async_copy(slot, slot, col_recv.at[phase, k]).wait()

    def mate_copy(phase, k, source, target):
        other = lax.rem(member + k, members)
        return pltpu.make_async_remote_copy(
            src_ref=source,
            dst_ref=target.at[member],
            send_sem=mate_send.at[phase, k],
            recv_sem=mate_recv.at[phase, members - k],
            device_id={"tile": mine * sub + other // size_w, "wave": lax.rem(other, size_w)},
            device_id_type=MESH,
        )

    def mate_wait(phase, k, target):
        slot = target.at[lax.rem(member + k, members)]
        pltpu.make_async_copy(slot, slot, mate_recv.at[phase, k]).wait()

    def halo_copies(phase, halo, edge):
        copies = []
        targets = ((down, w, 2), (down, other_w, 2), (up, w, 0), (up, other_w, 0), (t, other_w, 1))
        for number, (to_t, to_w, row) in enumerate(targets):
            own = number in (0, 2)
            copies.append(
                pltpu.make_async_remote_copy(
                    src_ref=halo.at[1, pl.ds(0, tiles)] if own else edge,
                    dst_ref=halo.at[row, pl.ds(0, tiles) if own else pl.ds(tiles, 2)],
                    send_sem=halo_send.at[phase, number],
                    recv_sem=halo_recv.at[phase, number],
                    device_id={"tile": to_t, "wave": to_w},
                    device_id_type=MESH,
                )
            )
        return copies

    def put_halo(h, value, halo, edge):
        halo[1, h] = value
        if h in (0, tiles - 1):
            edge[h // (tiles - 1)] = value

    started = []

    def start(copy):
        copy.start()
        started.append(copy)

    row_id = lax.broadcasted_iota(jnp.int32, (rows, lanes), 0)
    upper = row_id < tiles
    sign = jnp.where(upper, -1.0, 1.0)

    def times_i(x):
        return pltpu.roll(x, tiles, 0) * sign

    loads[0].wait()
    loads[1].wait()
    offset_rows = jnp.concatenate([offsets[:, 0, :], offsets[:, 1, :]], 0)
    for h in range(tiles):
        rounded = []
        for c in range(2):
            value = residual[h, c]
            send_a[:, c * tiles + h, :] = value
            rounded.append(value.astype(bf16))
        put_halo(h, jnp.concatenate(rounded, 0), halo_1, edge_1)
    for v in range(vectors):
        send_a[v, rows : 2 * rows, :] = offset_rows

    low = lax.broadcasted_iota(jnp.int32, (8, lanes), 0).astype(f32) + 0.5
    count = jnp.where(upper, float(count_x), float(count_y))
    tile_row = (row_id - tiles + other_w * tiles).astype(f32)

    def harmonics(position, cos_8, sin_8):
        cos_b, sin_b = cos_sin(position * low)
        cosines = [cos_b, cos_b * cos_8 - sin_b * sin_8]
        sines = [sin_b, sin_b * cos_8 + cos_b * sin_8]
        twice = cos_8 + cos_8
        for series in (cosines, sines):
            for m in range(2, 8):
                series.append(twice * series[-1] - series[-2])
        return jnp.concatenate(cosines + sines, 0)

    def tables(k):
        u = turn(k)
        off = recv_a[u, rows : 2 * rows, :]
        strip = (u * sub + part).astype(f32)
        pos = (jnp.where(upper, strip, tile_row) + off) / count
        cos_p, sin_p = cos_sin(0.5 * (pos + pltpu.roll(pos, tiles, 0)))
        cos_8, sin_8 = cos_sin(8.0 * pos)
        phi[k, 0] = cos_p
        phi[k, 1] = sin_p
        given = []
        for h in range(tiles):
            tx = harmonics(*[jnp.broadcast_to(x[h : h + 1], (8, lanes)) for x in (pos, cos_8, sin_8)])
            table_x[k, h] = tx.astype(bf16)
            row = tiles + h
            ty = harmonics(
                *[jnp.broadcast_to(x[row : row + 1], (8, lanes)) for x in (pos, cos_8, sin_8)]
            )
            table_y[k, h] = ty.astype(bf16)
            wide_y[k, h] = ty
            given.append(ty.astype(bf16))
        return given

    def add(totals, terms):
        return terms if totals is None else [x + y for x, y in zip(totals, terms)]

    def project(k, density, given=None):
        rotated = density * phi[k, 0] + times_i(density) * phi[k, 1]
        twisted = []
        for h in range(tiles):
            ty = table_y[k, h] if given is None else given[h]
            both = []
            for c in range(2):
                row = c * tiles + h
                q = jnp.broadcast_to(rotated[row : row + 1], (16, lanes)).astype(bf16)
                both.append(ty * jnp.concatenate([q] * (modes_y // 16), 0))
            twisted.append(jnp.concatenate(both, 0))
        return [
            rows_dot(
                jnp.concatenate(twisted[h : h + 2], 1),
                jnp.concatenate([table_x[k, h], table_x[k, h + 1]], 1),
            )
            for h in range(0, tiles, 2)
        ]

    def both_sums(totals):
        halves[w] = totals[0]
        halves[other_w] = totals[1]
        return halves[0] + halves[1]

    def weigh(total):
        x_r, y_r = total[0:half_y], total[half_y:modes_y]
        x_i, y_i = total[modes_y : modes_y + half_y], total[modes_y + half_y :]
        rx_r, ry_r, rx_i, ry_i = [pltpu.roll(x, half_x, 1) for x in (x_r, y_r, x_i, y_i)]
        f_0 = fact[0:half_y, 0:modes_x]
        f_s = fact[0:half_y, modes_x:]
        f_t = fact[half_y:, 0:modes_x]
        f_1 = fact[half_y:, modes_x:]
        matrix = jnp.concatenate(
            [
                f_0 * x_r + f_1 * ry_r - f_s * rx_i + f_t * y_i,
                f_0 * y_r - f_1 * rx_r - f_t * x_i - f_s * ry_i,
                f_0 * x_i + f_1 * ry_i + f_s * rx_r - f_t * y_r,
                f_0 * y_i - f_1 * rx_i + f_t * x_r + f_s * ry_r,
            ],
            0,
        ).astype(bf16)
        coeffs[w] = matrix
        coeffs[other_w] = matrix

    def expand(k):
        for h in range(0, tiles, 2):
            summed = jnp.dot(
                coeffs[(w, other_w)[h // 2]],
                jnp.concatenate([table_x[k, h], table_x[k, h + 1]], 1),
                preferred_element_type=f32,
            )
            for side in range(2):
                cols = slice(side * lanes, (side + 1) * lanes)
                ty = wide_y[k, h + side]
                for c in range(2):
                    row = c * tiles + h + side
                    far[k, row : row + 1, :] = jnp.sum(
                        summed[c * modes_y : (c + 1) * modes_y, cols] * ty, 0, keepdims=True
                    )
        value = far[k]
        return value * phi[k, 0] - times_i(value) * phi[k, 1]

    def near_field(halo):
        result = []
        for h in range(tiles):
            picked = []
            for j in range(9):
                slot = neighbor[0, h, j]
                row = slot // 3
                column = lax.rem(h + lax.rem(slot, 3) + tiles + 1, tiles + 2)
                picked.append(halo[row, column])
            left = jnp.concatenate(picked, 1)
            right = jnp.concatenate(
                [
                    jnp.concatenate([kernel_vmem[h, j, c] for j in range(9)], 0)
                    for c in range(2)
                ],
                1,
            )
            product = jnp.dot(left, right, preferred_element_type=f32)
            result.append(
                (
                    product[:vectors, :lanes] - product[vectors:, lanes:],
                    product[:vectors, lanes:] + product[vectors:, :lanes],
                )
            )
        return result

    pl.semaphore_wait(barrier, greeted)
    copies_1 = halo_copies(0, halo_1, edge_1)
    for copy in copies_1:
        start(copy)
    for k in reversed(range(vectors)):
        start(column_copy(phase_a, k, send_a.at[turn(k)], recv_a))

    for load in loads[2:6]:
        load.wait()
    my_weight = weight_vmem[frequency[mine]] * (1.0 / math.sqrt(modes_x * modes_y * panels))
    diagonal = jnp.sum(jnp.sum(my_weight, 0, keepdims=True), 1, keepdims=True)
    exact = lax.Precision.HIGHEST

    def pick(lattice, half):
        index = lax.broadcasted_iota(jnp.int32, (half, 2 * half), 0)
        given = jnp.broadcast_to(lattice[...], index.shape)
        plus = jnp.where(given == index + half, 1.0, 0.0)
        minus = jnp.where(given == half - 1 - index, 1.0, 0.0)
        return plus + minus, plus - minus

    even_y, odd_y = pick(lattice_y, half_y)
    even_x, odd_x = pick(lattice_x, half_x)
    by_y = rows_dot(jnp.concatenate([even_y, odd_y], 0), my_weight, exact)
    pick_x = jnp.concatenate([even_x, even_x, -odd_x, odd_x], 0)
    fact[...] = rows_dot(by_y, pick_x, exact)

    ahead = vectors // 2
    total = None

    def take(k):
        nonlocal total
        column_wait(phase_a, k, recv_a)
        given = tables(k)
        dense[k] = recv_a[turn(k), 0:rows, :].astype(bf16).astype(f32)
        total = add(total, project(k, dense[k], given))

    for k in range(ahead):
        take(k)

    def send_tiles(pairs, slab):
        for h in range(tiles):
            for c in range(2):
                slab[:, c * tiles + h, :] = pairs[h][c]

    for load in loads[6:]:
        load.wait()
    for copy in copies_1:
        copy.wait_recv()
    send_tiles(near_field(halo_1), send_n)
    for k in reversed(range(vectors)):
        start(column_copy(phase_n, k, send_n.at[turn(k)], recv_n))

    for k in range(ahead, vectors):
        take(k)

    def gather_sum(phase, source, target):
        if members == 2:
            return source[...] + target[lax.rem(member + 1, members)]
        target[member] = source[...]
        return jnp.sum(target[...], 0)

    send_g1[...] = both_sums(total)
    for k in range(1, members):
        start(mate_copy(0, k, send_g1, recv_g1))
    for k in range(1, members):
        mate_wait(0, k, recv_g1)
    weigh(gather_sum(0, send_g1, recv_g1))

    fields = [expand(k) for k in range(vectors)]
    def halo_message(k):
        u = turn(k)
        before = zeta[lax.rem(u + vectors - 1, vectors)]
        own = zeta[u]
        after = zeta[lax.rem(u + 1, vectors)]
        rounded = jnp.concatenate([before, own, after, after], 0).astype(bf16)
        send_h[k] = rounded
        start(column_copy(phase_h, k, send_h.at[k], recv_h))
        inner = (row_id == 1) | (row_id == tiles + 1)
        edge = inner | (row_id == tiles - 2) | (row_id == 2 * tiles - 2)
        moved = jnp.where(inner, pltpu.roll(own, 1, 0), pltpu.roll(own, 2 * tiles - 1, 0))
        rounded = jnp.concatenate([jnp.where(edge, moved, before), after], 0).astype(bf16)
        if k:
            send_o[k] = rounded
            start(column_copy(phase_o, k, send_o.at[k], recv_o, w))
        else:
            recv_o[mine] = rounded

    zero = jnp.zeros((rows, lanes), f32)
    sums = [zero] * 5
    total = None
    for k in range(vectors):
        column_wait(phase_n, k, recv_n)
        u = turn(k)
        given = recv_a[u, 0:rows, :]
        base = dense[k]
        value = fields[k] + recv_n[u] - diagonal * base
        zeta[u] = value
        turned = times_i(value)
        terms = (given * given, base * base, base * value, -base * turned, value * value)
        sums = [x + y for x, y in zip(sums, terms)]
        if sub > 1:
            send_z[k] = value
            start(column_copy(phase_z, k, send_z.at[k], recv_z))
        if sub == 1 and k == vectors - 1:
            for other in reversed(range(2, vectors)):
                halo_message(other)
        total = add(total, project(k, value))
    send_g2[0 : 2 * modes_y] = both_sums(total)
    line = jnp.zeros((rows, lanes), f32)
    for number, x in enumerate(sums):
        whole = jnp.sum(jnp.sum(x, 0, keepdims=True), 1, keepdims=True)
        line = jnp.where(row_id == number, whole, line)
    send_g2[2 * modes_y :] = line
    for k in range(1, members):
        start(mate_copy(1, k, send_g2, recv_g2))
    if sub == 1:
        for k in (1, 0):
            halo_message(k)

    if sub > 1:
        for k in range(vectors):
            column_wait(phase_z, k, recv_z)
        for h in range(tiles):
            pair = [recv_z[:, c * tiles + h, :].astype(bf16) for c in range(2)]
            put_halo(h, jnp.concatenate(pair, 0), halo_2, edge_2)
        copies_2 = halo_copies(1, halo_2, edge_2)
        for copy in copies_2:
            start(copy)

    for k in range(1, members):
        mate_wait(1, k, recv_g2)
    total = gather_sum(1, send_g2, recv_g2)
    weigh(total[0 : 2 * modes_y])
    line = total[2 * modes_y :]
    squares, base_sq, inner_r, inner_i, value_sq = [line[i : i + 1] for i in range(5)]
    shift = 0.5 + diagonal
    variance = squares / panels + eps_norm
    scale = jnp.sqrt(variance)
    over = 1.0 / (panels * variance)
    rest_r = (shift * base_sq + inner_r) * over
    coef_i = inner_i * over
    coef_r = rest_r
    move_r = coef_r - shift
    update_sq = (
        value_sq
        - 2.0 * (move_r * inner_r + coef_i * inner_i)
        + (move_r * move_r + coef_i * coef_i) * base_sq
    )
    update_scale = jnp.sqrt(jnp.maximum(update_sq, 0.0) * over + eps_norm)
    inverse = 1.0 / (scale * update_scale)
    lane_id = lax.broadcasted_iota(jnp.int32, (1, lanes), 1)
    result = jnp.zeros((1, lanes), f32)
    for number, x in enumerate((scale, coef_r, coef_i, update_scale, inverse)):
        result = jnp.where(lane_id == number, x, result)
    result = jnp.broadcast_to(result, (rows, lanes))

    order = list(reversed(range(vectors)))
    field = expand(order[0])
    for number, k in enumerate(order):
        u = turn(k)
        if number and number + 1 < vectors:
            coming = expand(order[number + 1])
        value = zeta[u]
        image = value + shift * dense[k]
        out = field + 0.5 * value - move_r * image - coef_i * times_i(image)
        send_f[u, 0:rows, :] = out * inverse
        send_f[u, rows : 2 * rows, :] = result
        start(column_copy(phase_f, k, part_of(phase_f, send_f, u), recv_f))
        field = coming if number else expand(order[1])

    last = started[-vectors:]
    for copy in started[:-vectors]:
        copy.wait_send()
    if sub > 1:
        for copy in copies_2:
            copy.wait_recv()
    else:
        for k in range(vectors):
            column_wait(phase_h, k, recv_h)
            if k:
                column_wait(phase_o, k, recv_o)
        near_h[...] = recv_h[...].astype(f32)
        near_o[...] = recv_o[...].astype(f32)
        for strip in range(3):
            for h in range(tiles):
                first = strip * rows + h
                pair = [near_h[:, first + c * tiles, :] for c in range(2)]
                halo_2[strip, h] = jnp.concatenate(pair, 0).astype(bf16)
            for h in (0, tiles - 1):
                first = (h, 1 if h == 0 else h - 1, rows + h)[strip]
                pair = [near_o[:, first + c * tiles, :] for c in range(2)]
                halo_2[strip, tiles + h // (tiles - 1)] = jnp.concatenate(pair, 0).astype(bf16)
    near = near_field(halo_2)
    for k in range(vectors):
        column_wait(phase_f, k, recv_f)
    row = lax.broadcasted_iota(jnp.int32, (vectors, lanes), 0)
    lane = lax.broadcasted_iota(jnp.int32, (vectors, lanes), 1)
    scalars = recv_f[:, rows, :]
    columns = [
        jnp.sum(jnp.where(lane == number, scalars, 0.0), 1, keepdims=True) for number in range(5)
    ]
    scaling = columns[4]
    for h in range(tiles):
        for c in range(2):
            image_out[h, c] = recv_f[:, c * tiles + h, :] + near[h][c] * scaling
    for number in range(4):
        line = jnp.sum(jnp.where(row == lane, columns[number], 0.0), 0, keepdims=True)
        arnoldi_out[number : number + 1, :] = line[:, :vectors]

    for copy in last:
        copy.wait_send()


def hand_over(image, arnoldi, image_out, arnoldi_out):
    image_out[...] = image[...]
    arnoldi_out[...] = arnoldi[...]


def per_device(
    size_t,
    size_w,
    residual,
    kernel,
    offsets,
    neighbor,
    frequency,
    lattice_x,
    lattice_y,
    spectral_weight,
):
    strips, tiles, _, vectors, lanes = residual.shape
    modes_x, modes_y = spectral_weight.shape[1:]
    assert strips == 1 and lanes == 128 and size_w == 2 and size_t > 2
    assert size_t % vectors == 0 and tiles == 4 and vectors == 8
    assert modes_x == 128 and modes_y == 128
    members = size_w * (size_t // vectors)
    rows = 2 * tiles
    vmem = pl.BlockSpec(memory_space=pltpu.VMEM)
    anywhere = pl.BlockSpec(memory_space=pl.ANY)
    halo = pltpu.VMEM((3, tiles + 2, 2 * vectors, lanes), bf16)
    edge = pltpu.VMEM((2, 2 * vectors, lanes), bf16)
    wide = pltpu.VMEM((vectors, 2 * rows, lanes), f32)
    slim = pltpu.VMEM((vectors, rows, lanes), f32)
    image, arnoldi = pl.pallas_call(
        functools.partial(body, size_t, size_w, tiles, vectors, modes_x, modes_y),
        out_shape=(
            pltpu.VMEM((tiles, 2, vectors, lanes), f32),
            pltpu.VMEM((4, vectors), f32),
        ),
        in_specs=[anywhere] * 8,
        out_specs=(vmem, vmem),
        scratch_shapes=[
            wide,
            wide,
            slim,
            slim,
            slim,
            slim,
            pltpu.VMEM((vectors, 4 * rows, lanes), bf16),
            pltpu.VMEM((vectors, 4 * rows, lanes), bf16),
            pltpu.VMEM((vectors, 2 * rows, lanes), bf16),
            pltpu.VMEM((vectors, 2 * rows, lanes), bf16),
            pltpu.VMEM((vectors, 4 * rows, lanes), f32),
            wide,
            wide,
            wide,
            pltpu.VMEM((2 * modes_y, modes_x), f32),
            pltpu.VMEM((members, 2 * modes_y, modes_x), f32),
            pltpu.VMEM((2 * modes_y + rows, modes_x), f32),
            pltpu.VMEM((members, 2 * modes_y + rows, modes_x), f32),
            halo,
            halo,
            edge,
            edge,
            pltpu.VMEM((vectors, tiles, modes_x, lanes), bf16),
            pltpu.VMEM((vectors, tiles, modes_y, lanes), bf16),
            pltpu.VMEM((vectors, tiles, modes_y, lanes), f32),
            pltpu.VMEM((vectors, 2, rows, lanes), f32),
            slim,
            slim,
            slim,
            pltpu.VMEM((modes_y, 2 * modes_x), f32),
            pltpu.VMEM((2, 2 * modes_y, modes_x), bf16),
            pltpu.VMEM((2, 2 * modes_y, modes_x), f32),
            pltpu.VMEM(residual.shape[1:], f32),
            pltpu.VMEM(offsets.shape[1:], f32),
            pltpu.SMEM(neighbor.shape, jnp.int32),
            pltpu.SMEM(frequency.shape, jnp.int32),
            pltpu.VMEM((1, modes_x), jnp.int32),
            pltpu.VMEM((1, modes_y), jnp.int32),
            pltpu.VMEM((tiles, 9, 2, lanes, lanes), bf16),
            pltpu.VMEM(spectral_weight.shape, f32),
            pltpu.SemaphoreType.DMA((8,)),
            pltpu.SemaphoreType.DMA((6, vectors)),
            pltpu.SemaphoreType.DMA((6, vectors)),
            pltpu.SemaphoreType.DMA((2, members)),
            pltpu.SemaphoreType.DMA((2, members)),
            pltpu.SemaphoreType.DMA((2, 5)),
            pltpu.SemaphoreType.DMA((2, 5)),
        ],
        compiler_params=pltpu.CompilerParams(
            collective_id=0, has_side_effects=True, vmem_limit_bytes=56 * 1024 * 1024
        ),
        name="arnoldi_pair",
    )(
        residual[0],
        kernel[0],
        offsets[0],
        neighbor,
        frequency,
        lattice_x[None],
        lattice_y[None],
        spectral_weight,
    )
    image, arnoldi = [
        pltpu.with_memory_space_constraint(x, pltpu.VMEM) for x in (image, arnoldi)
    ]
    image, arnoldi = pl.pallas_call(
        hand_over,
        out_shape=(
            jax.ShapeDtypeStruct(image.shape, f32),
            jax.ShapeDtypeStruct(arnoldi.shape, f32),
        ),
        in_specs=[vmem, vmem],
        out_specs=(vmem, vmem),
        name="hand_over",
    )(image, arnoldi)
    return image[None], arnoldi


def solution(mesh):
    return jax.shard_map(
        functools.partial(per_device, mesh.shape["tile"], mesh.shape["wave"]),
        mesh=mesh,
        in_specs=(
            P(("grp", "tile"), "wave", None, None, None),
            P(("grp", "tile"), "wave", None, None, None, None),
            P(("grp", "tile"), "wave", None, None),
            P(("grp", "tile"), "wave", None),
            P("grp"),
            P(),
            P(),
            P(),
        ),
        out_specs=(P(("grp", "tile"), "wave", None, None, None), P("grp", None)),
        check_vma=False,
    )
```
